256 devices in a mesh: pair: 64 (over y, z, core), batch: 4 (over x).
Axes of the slice: x: 4, y: 4, z: 8, core: 2. Of those that a mesh axis runs over, the one named last changes fastest.
Arguments:
- ao_ints: bfloat16 [32768, 4096], P('pair', 'batch'), may hold values from -6 to 6
- shell_mask: int32 [512, 64], P('pair', 'batch'), may hold values 0 or 1
- bra_shells: int32 [512, 2], replicated, may hold values from 0 to 749
- ket_shells: int32 [64, 2], P('batch'), may hold values from 0 to 749
- mo_coeff: bfloat16 [6000, 256], replicated, may hold values from -0.59765625 to 0.59765625
- mo_ranges: int32 [4], replicated, may hold values from 0 to 192
Outputs:
- transformed: float32 [4096, 1024], P(('pair', 'batch'))
The draws below stay inside these ranges and needn't reach their ends.
All inputs are finite; a program needn't handle non-finite values. No bound on the sum of `shell_mask` on one device may be relied on, other than what follows from the above.
Results may differ from the reference program's by a relative error of at most 0.0049.
Values may be sent and summed in bfloat16 or wider, within the bound.
A program may use at most 64 MiB of HBM per device.

```python
import jax
import jax.numpy as jnp
from jax import lax

NBF = 6000
SHELL = 8
NORB = 256
NI = 64
NA = 32
KET_SP = 16
NSHELL = 750
BRA_PAIRS = 512
KET_PAIRS = 64
BRA = 32768
KET = 4096
N_BATCH = 4


def set_ends(drawn, rng, least, top_value):
    dims = drawn.shape
    place = [jax.random.randint(jax.random.fold_in(rng, axis), (), 0, dims[axis]) for axis in range(len(dims))]
    drawn = drawn.at[tuple(place)].set(least)
    longest = dims.index(max(dims))
    place[longest] = (place[longest] + 1) % dims[longest]
    return drawn.at[tuple(place)].set(top_value)


def block_levels(own_key, shape, cuts, least, top_value):
    loudness = 1.0
    for dim, blocks in cuts:
        draws = jax.random.uniform(jax.random.fold_in(jax.random.fold_in(own_key, 6), dim), (blocks,), jnp.float32, least / len(cuts), top_value / len(cuts))
        loudness = loudness * jnp.repeat(jnp.exp(draws), shape[dim] // blocks).reshape((-1,) + (1,) * (len(shape) - 1 - dim))
    return loudness


def normal_values(rng, extent, scale, limit, split=(), held_as=jnp.bfloat16):
    gain = block_levels(rng, extent, split, -0.22, 0.18) if split else 1.0
    entries = jax.random.normal(rng, extent, jnp.float32) * scale * gain
    return jnp.minimum(jnp.maximum(entries, -limit), limit).astype(held_as)


def setup_inputs(seed: int = 0) -> dict:
    key_of = jax.random.split(jax.random.key(seed), 7)
    ao_ints = normal_values(key_of[0], (BRA, KET), 1.0, 6.0, ((0, 64), (1, 4)))
    shell_mask = set_ends((jax.random.randint(key_of[1], (BRA_PAIRS, KET_PAIRS), 0, 4) < 3).astype(jnp.int32), jax.random.fold_in(key_of[1], 1), 0, 1)
    bra_shells = set_ends(jax.random.randint(key_of[2], (BRA_PAIRS, 2), 0, NSHELL), jax.random.fold_in(key_of[2], 1), 0, NSHELL - 1).astype(jnp.int32)
    ket_shells = set_ends(jax.random.randint(key_of[3], (KET_PAIRS, 2), 0, NSHELL), jax.random.fold_in(key_of[3], 1), 0, NSHELL - 1).astype(jnp.int32)
    mo_coeff = normal_values(key_of[4], (NBF, NORB), 0.1, 0.59765625)
    mo_ranges = set_ends(jax.random.randint(key_of[5], (4,), 0, NORB - NI + 1), jax.random.fold_in(key_of[5], 1), 0, NORB - NI).astype(jnp.int32)
    return {"ao_ints": ao_ints, "shell_mask": shell_mask, "bra_shells": bra_shells, "ket_shells": ket_shells, "mo_coeff": mo_coeff, "mo_ranges": mo_ranges}


def window_cols(mo_coeff, start, count):
    picked = lax.dynamic_slice_in_dim(mo_coeff, start, count, 1)
    return picked.reshape(mo_coeff.shape[0] // SHELL, SHELL, count)


def outer_rows(first_cols, second_cols, shells):
    rows_one = jnp.take(first_cols, shells[:, 0], axis=0).astype(jnp.float32)
    rows_two = jnp.take(second_cols, shells[:, 1], axis=0).astype(jnp.float32)
    product = rows_one[:, :, None, :, None] * rows_two[:, None, :, None, :]
    shell_size = first_cols.shape[1]
    return product.reshape(shells.shape[0] * shell_size * shell_size, first_cols.shape[2] * second_cols.shape[2]).astype(jnp.bfloat16)


def reference(ao_ints, shell_mask, bra_shells, ket_shells, mo_coeff, mo_ranges):
    ket_coeff = outer_rows(window_cols(mo_coeff, mo_ranges[0], NI), window_cols(mo_coeff, mo_ranges[1], NI), ket_shells)
    bra_coeff = outer_rows(window_cols(mo_coeff, mo_ranges[2], NA), window_cols(mo_coeff, mo_ranges[3], NA), bra_shells)
    bra_count = shell_mask.shape[0]
    ket_count = shell_mask.shape[1]
    block_mask = shell_mask.astype(ao_ints.dtype)
    screened = (ao_ints.reshape(bra_count, SHELL * SHELL, ket_count, SHELL * SHELL) * block_mask[:, None, :, None]).reshape(ao_ints.shape)
    ket_rows = KET_SP * SHELL * SHELL
    half_sum = jnp.zeros((ao_ints.shape[0], NI * NI), jnp.float32)
    for batch_index in range(N_BATCH):
        columns = screened[:, batch_index * ket_rows:(batch_index + 1) * ket_rows].astype(jnp.float32)
        coeff_rows = ket_coeff[batch_index * ket_rows:(batch_index + 1) * ket_rows].astype(jnp.float32)
        halfway = jnp.dot(columns, coeff_rows, precision=lax.Precision.HIGHEST, preferred_element_type=jnp.float32).astype(jnp.bfloat16)
        half_sum = half_sum + halfway.astype(jnp.float32)
    return jnp.dot(half_sum.T, bra_coeff.astype(jnp.float32), precision=lax.Precision.HIGHEST, preferred_element_type=jnp.float32)
```

```python
import jax
import jax.numpy as jnp
from jax import lax
from jax.sharding import PartitionSpec as P

SHELL = 8
NI = 64
NA = 32


def shell_rows(mo_coeff, shells, start, count):
    table = mo_coeff.reshape(mo_coeff.shape[0] // SHELL, SHELL, mo_coeff.shape[1])
    rows = jnp.take(table, shells, axis=0)
    return lax.dynamic_slice_in_dim(rows, start, count, 2)


def on_device(ao_ints, shell_mask, bra_shells, ket_shells, mo_coeff, mo_ranges):
    local_bra = shell_mask.shape[0]
    local_ket = shell_mask.shape[1]
    pair_count = lax.axis_size("pair")
    batch_count = lax.axis_size("batch")
    place = lax.axis_index("pair")
    own_shells = lax.dynamic_slice_in_dim(bra_shells, place * local_bra, local_bra, 0)
    bra_one = shell_rows(mo_coeff, own_shells[:, 0], mo_ranges[2], NA)
    bra_two = shell_rows(mo_coeff, own_shells[:, 1], mo_ranges[3], NA)
    bra_coeff = (
        bra_one.astype(jnp.float32)[:, :, None, :, None] * bra_two.astype(jnp.float32)[:, None, :, None, :]
    ).reshape(local_bra * SHELL * SHELL, NA * NA).astype(jnp.bfloat16)
    block_mask = shell_mask.astype(jnp.bfloat16)
    screened = (
        ao_ints.reshape(local_bra, SHELL * SHELL, local_ket, SHELL * SHELL) * block_mask[:, None, :, None]
    ).reshape(ao_ints.shape)
    partial = lax.dot_general(
        bra_coeff, screened, (((0,), (0,)), ((), ())), preferred_element_type=jnp.float32
    )
    bra_done = lax.psum_scatter(partial, "pair", scatter_dimension=0, tiled=True)
    own_ab = bra_done.shape[0]
    ket_one = shell_rows(mo_coeff, ket_shells[:, 0], mo_ranges[0], NI)
    ket_two = shell_rows(mo_coeff, ket_shells[:, 1], mo_ranges[1], NI)
    ket_coeff = (
        ket_one.astype(jnp.float32)[:, :, None, :, None] * ket_two.astype(jnp.float32)[:, None, :, None, :]
    ).reshape(local_ket * SHELL * SHELL, NI * NI).astype(jnp.bfloat16)
    both = jnp.dot(bra_done.astype(jnp.bfloat16), ket_coeff, preferred_element_type=jnp.float32)
    split = both.reshape(own_ab, NI, batch_count, NI // batch_count)
    summed = lax.psum_scatter(split.transpose(2, 1, 3, 0), "batch", scatter_dimension=0, tiled=True)
    summed = summed.reshape(pair_count, NI // batch_count, own_ab)
    return lax.all_to_all(summed, "pair", split_axis=0, concat_axis=2, tiled=True).reshape(NI // batch_count, NA * NA)


def solution(mesh):
    return jax.shard_map(
        on_device,
        mesh=mesh,
        in_specs=(P("pair", "batch"), P("pair", "batch"), P(), P("batch", None), P(), P()),
        out_specs=P(("pair", "batch"), None),
        check_vma=False,
    )
```

```python
import jax
import jax.numpy as jnp
from jax import lax
from jax.experimental import pallas as pl
from jax.experimental.pallas import tpu as pltpu
from jax.sharding import PartitionSpec as P

SHELL = 8
NX, NY, NZ, NC = 4, 4, 8, 2
OWN = 16
MESH = pl.DeviceIdType.MESH
BF = jnp.bfloat16
F32 = jnp.float32


def iota(shape, dim):
    return lax.broadcasted_iota(jnp.int32, shape, dim)


def where_one(condition):
    return jnp.where(condition, 1.0, 0.0).astype(BF)


def dot(a, b):
    return jnp.dot(a, b, preferred_element_type=F32)


def dot_last(a, b):
    return lax.dot_general(a, b, (((1,), (1,)), ((), ())), preferred_element_type=F32)


def pair_id(y, z, c):
    return (y * NZ + z) * NC + c


def kernel(
    ao_hbm, mask_ref, bra_ref, ket_ref, mo_hbm, ranges_ref, out_ref,
    ao_own, ao_other, mask_other, mo_table, bra_one, bra_two, ket_one, ket_two,
    bra_t, partial, to_y, from_y, to_z, from_z, own_sum, ket_wide, ket_narrow,
    spread, quarter, to_xy, from_xy, to_zc, from_zc,
    load_sem, core_send, core_recv, y_send, y_recv, z_send, z_recv, xy_send, xy_recv, zc_send, zc_recv,
):
    place = lax.axis_index("pair")
    x = lax.axis_index("batch")
    c = lax.rem(place, NC)
    z = lax.rem(place // NC, NZ)
    y = place // (NC * NZ)

    def plane_peer(dx, dy):
        return (pair_id(lax.rem(y + dy, NY), z, c), lax.rem(x + dx, NX))

    def line_peer(dz, dc):
        return (pair_id(y, lax.rem(z + dz, NZ), lax.rem(c + dc, NC)), x)

    load_ao = pltpu.make_async_copy(ao_hbm, ao_own, load_sem.at[0])
    load_mo = pltpu.make_async_copy(mo_hbm, mo_table, load_sem.at[1])
    load_mo.start()
    load_ao.start()
    barrier = pltpu.get_barrier_semaphore()
    plane = [(dx, dy) for dx in range(NX) for dy in range(NY) if dx or dy]
    line = [(dz, dc) for dz in range(NZ) for dc in range(NC) if dz or dc]
    for dx, dy in plane:
        pl.semaphore_signal(barrier, inc=1, device_id=plane_peer(dx, dy), device_id_type=MESH)
    for dz, dc in line:
        pl.semaphore_signal(barrier, inc=1, device_id=line_peer(dz, dc), device_id_type=MESH)

    load_mo.wait()
    half = mask_ref.shape[0]
    first_pair = place * half
    other_pair = pair_id(y, z, lax.rem(c + 1, NC)) * half

    def take_bra(t, carry):
        spot = pl.ds(pl.multiple_of(t * SHELL, SHELL), SHELL)
        late = pl.ds(pl.multiple_of((half + t) * SHELL, SHELL), SHELL)
        bra_one[spot, :] = mo_table[bra_ref[first_pair + t, 0]].astype(F32)
        bra_two[spot, :] = mo_table[bra_ref[first_pair + t, 1]].astype(F32)
        bra_one[late, :] = mo_table[bra_ref[other_pair + t, 0]].astype(F32)
        bra_two[late, :] = mo_table[bra_ref[other_pair + t, 1]].astype(F32)
        return carry

    lax.fori_loop(0, half, take_bra, 0)

    def take_ket(s, carry):
        spot = pl.ds(pl.multiple_of(s * SHELL, SHELL), SHELL)
        ket_one[spot, :] = mo_table[ket_ref[s, 0]].astype(F32)
        ket_two[spot, :] = mo_table[ket_ref[s, 1]].astype(F32)
        return carry

    lax.fori_loop(0, ket_ref.shape[0], take_ket, 0)

    depth = bra_one.shape[0]
    width = bra_t.shape[1]
    orbitals = bra_one.shape[1]
    row = iota((bra_t.shape[0], orbitals), 0)
    piece = row >> 7
    to_z_place = (z + jnp.where(((row >> 4) & 1) == 0, 4 + piece, 3 - piece)) & (NZ - 1)
    to_y_place = (y + ((row >> 5) & 3)) & (NY - 1)
    ab = to_z_place * 128 + c * 64 + to_y_place * 16 + (row & 15)
    orbital = iota((bra_t.shape[0], orbitals), 1)
    pick_a = where_one(orbital == ranges_ref[2] + (ab >> 5))
    pick_b = where_one(orbital == ranges_ref[3] + (ab & 31))
    small_a = dot_last(pick_a, bra_one[...].astype(BF)).astype(BF)
    small_b = dot_last(pick_b, bra_two[...].astype(BF)).astype(BF)
    source = iota((depth, width), 0)
    column = iota((depth, width), 1)
    over_m = where_one(source == (column >> 3))
    over_n = where_one(((source >> 3) == (column >> 6)) & ((source & 7) == (column & 7)))
    for start in range(0, bra_t.shape[0], 128):
        rows = slice(start, start + 128)
        bra_t[rows, :] = (dot(small_a[rows], over_m) * dot(small_b[rows], over_n)).astype(BF)

    mask_spread = where_one(
        iota((mask_ref.shape[1], ao_own.shape[1]), 0) == (iota((mask_ref.shape[1], ao_own.shape[1]), 1) >> 6)
    )

    def screen(values, mask):
        wide = dot(mask[...].astype(F32).astype(BF), mask_spread).astype(BF)
        for t in range(half):
            block = slice(64 * t, 64 * t + 64)
            values[block, :] = values[block, :] * wide[t:t + 1, :]

    pl.semaphore_wait(barrier, len(plane) + len(line))

    ao_copy = pltpu.make_async_remote_copy(
        ao_hbm, ao_other, core_send.at[0], core_recv.at[0], device_id=line_peer(0, 1), device_id_type=MESH
    )
    mask_copy = pltpu.make_async_remote_copy(
        mask_ref, mask_other, core_send.at[1], core_recv.at[1], device_id=line_peer(0, 1), device_id_type=MESH
    )
    mask_copy.start()
    ao_copy.start()

    load_ao.wait()
    screen(ao_own, mask_ref)
    own_width = ao_own.shape[0]

    def own_part(p, carry):
        rows = pl.ds(pl.multiple_of(p * 128, 128), 128)
        partial[rows, :] = dot(bra_t[rows, :own_width], ao_own[...])
        return carry

    lax.fori_loop(0, 4, own_part, 0)
    mask_copy.wait_recv()
    ao_copy.wait_recv()
    screen(ao_other, mask_other)

    def y_copy(p, dy):
        return pltpu.make_async_remote_copy(
            to_y.at[p, dy - 1], from_y.at[p, dy - 1], y_send.at[p, dy - 1], y_recv.at[p, dy - 1],
            device_id=plane_peer(0, dy), device_id_type=MESH,
        )

    def other_part(p, carry):
        rows = pl.ds(pl.multiple_of(p * 128, 128), 128)
        total = partial[rows, :] + dot(bra_t[rows, own_width:], ao_other[...])
        own_sum[p] = total[:32]
        for dy in (2, 1, 3):
            to_y[p, dy - 1] = total[32 * dy:32 * dy + 32].astype(BF)
            y_copy(p, dy).start()
        return carry

    lax.fori_loop(0, 4, other_part, 0)

    columns = spread.shape[1]
    col = iota((orbitals, columns), 1)
    first = (((y + (col >> 8)) & (NY - 1)) << 4) + (((z + ((col >> 5) & 7)) & (NZ - 1)) << 1) + ((c + (col >> 4)) & 1)
    pick_i = where_one(iota((orbitals, columns), 0) == ranges_ref[0] + first)
    spread[...] = dot(ket_one[...].astype(BF), pick_i)
    j_row = iota((ket_narrow.shape[0], orbitals), 0)
    second = (((x + (j_row >> 4)) & (NX - 1)) << 4) + (j_row & 15)
    pick_j = where_one(iota((ket_narrow.shape[0], orbitals), 1) == ranges_ref[1] + second)
    narrow = dot_last(pick_j, ket_two[...].astype(BF)).astype(BF)
    ket_narrow[...] = jnp.concatenate([narrow, narrow], axis=1)

    def z_copy(dz):
        return pltpu.make_async_remote_copy(
            to_z.at[dz - 1], from_z.at[dz - 1], z_send.at[dz - 1], z_recv.at[dz - 1],
            device_id=line_peer(dz, 0), device_id_type=MESH,
        )

    summed = None
    for p in range(4):
        for dy in range(1, NY):
            y_copy(p, dy).wait_recv()
        total = own_sum[p] + from_y[p, 0].astype(F32) + from_y[p, 1].astype(F32) + from_y[p, 2].astype(F32)
        for part, dz in ((total[:16], 4 + p), (total[16:], 3 - p)):
            if dz == 0:
                summed = part
            else:
                to_z[dz - 1] = part.astype(BF)
                z_copy(dz).start()
    for dz in (1, 7, 2, 6, 3, 5, 4):
        z_copy(dz).wait_recv()
        summed = summed + from_z[dz - 1].astype(F32)

    high = summed.astype(BF)
    low = (summed - high.astype(F32)).astype(BF)
    lanes = where_one((iota((2 * OWN, 128), 0) & 15) == (iota((2 * OWN, 128), 1) & 15))
    ket_wide[...] = lax.dot_general(
        jnp.concatenate([high, low], axis=0), lanes, (((0,), (0,)), ((), ())), preferred_element_type=F32
    )

    def over_first(s, carry):
        sums = [None] * (columns // 128)
        factors = spread[pl.ds(pl.multiple_of(s * SHELL, SHELL), SHELL), :]
        for m in range(SHELL):
            block = ket_wide[pl.ds(pl.multiple_of((s * SHELL + m) * SHELL, SHELL), SHELL), :]
            for tile in range(columns // 128):
                term = factors[m:m + 1, 128 * tile:128 * tile + 128] * block
                sums[tile] = term if m == 0 else sums[tile] + term
        for tile in range(columns // 128):
            quarter[pl.ds(pl.multiple_of(s * SHELL, SHELL), SHELL), 128 * tile:128 * tile + 128] = sums[tile]
        return carry

    lax.fori_loop(0, spread.shape[0] // SHELL, over_first, 0)
    value = quarter[...]
    value_high = value.astype(BF)
    value_low = (value - value_high.astype(F32)).astype(BF)
    both = dot(ket_narrow[...], jnp.concatenate([value_high, value_low], axis=0))

    def plane_copy(dx, dy, slot):
        return pltpu.make_async_remote_copy(
            to_xy.at[dx, dy], from_xy.at[slot[0], slot[1]], xy_send.at[dx * NY + dy], xy_recv.at[dx * NY + dy],
            device_id=plane_peer(dx, dy), device_id_type=MESH,
        )

    for dx, dy in sorted(plane, key=lambda d: -min(d[0], NX - d[0]) - min(d[1], NY - d[1])):
        to_xy[dx, dy] = both[16 * dx:16 * dx + 16, 256 * dy:256 * dy + 256]
        plane_copy(dx, dy, (y, x)).start()
    from_xy[y, x] = both[:16, :256]
    for dx, dy in plane:
        plane_copy(dx, dy, (lax.rem(y + NY - dy, NY), lax.rem(x + NX - dx, NX))).wait_recv()
    merged = [from_xy[k, 0] + from_xy[k, 1] + from_xy[k, 2] + from_xy[k, 3] for k in range(NY)]

    def line_copy(dz, dc, slot):
        return pltpu.make_async_remote_copy(
            to_zc.at[dz * NC + dc], from_zc.at[slot[0], slot[1]], zc_send.at[dz * NC + dc], zc_recv.at[dz * NC + dc],
            device_id=line_peer(dz, dc), device_id_type=MESH,
        )

    lane = iota((8, 128), 1)
    for dz, dc in sorted([(dz, dc) for dz in range(NZ) for dc in range(NC)], key=lambda d: -min(d[0], NZ - d[0])):
        group = dz * NC + dc
        tile = slice(128 * (group // 8), 128 * (group // 8) + 128)
        message = None
        for k in range(8):
            block = merged[k % 4][8 * (k // 4):8 * (k // 4) + 8, tile]
            shift = (16 * k - 16 * (group % 8)) % 128
            moved = pltpu.roll(block, shift, 1) if shift else block
            message = moved if message is None else jnp.where((lane >> 4) == k, moved, message)
        if group:
            to_zc[group] = message
            line_copy(dz, dc, (z, c)).start()
        else:
            from_zc[z, c] = message
    for dz, dc in line:
        line_copy(dz, dc, (lax.rem(z + NZ - dz, NZ), lax.rem(c + NC - dc, NC))).wait_recv()
    for k in range(NZ):
        left, right = from_zc[k, 0], from_zc[k, 1]
        out_ref[0:8, 128 * k:128 * k + 128] = jnp.where(lane < 64, left, pltpu.roll(right, 64, 1))
        out_ref[8:16, 128 * k:128 * k + 128] = jnp.where(lane < 64, pltpu.roll(left, 64, 1), right)

    mask_copy.wait_send()
    ao_copy.wait_send()
    for p in range(4):
        for dy in range(1, NY):
            y_copy(p, dy).wait_send()
    for dz in range(1, NZ):
        z_copy(dz).wait_send()
    for dx, dy in plane:
        plane_copy(dx, dy, (y, x)).wait_send()
    for dz, dc in line:
        line_copy(dz, dc, (z, c)).wait_send()


def on_device(ao_ints, shell_mask, bra_shells, ket_shells, mo_coeff, mo_ranges):
    table = mo_coeff.reshape(mo_coeff.shape[0] // SHELL, SHELL, mo_coeff.shape[1])
    rows, cols = ao_ints.shape
    orbitals = mo_coeff.shape[1]
    ket_rows = ket_shells.shape[0] * SHELL
    bra_rows = NC * shell_mask.shape[0] * SHELL
    dma = pltpu.SemaphoreType.DMA
    whole = pl.BlockSpec(memory_space=pl.ANY)
    scalar = pl.BlockSpec(memory_space=pltpu.SMEM)
    vector = pl.BlockSpec(memory_space=pltpu.VMEM)
    return pl.pallas_call(
        kernel,
        out_shape=jax.ShapeDtypeStruct((16, 1024), F32),
        in_specs=[whole, vector, scalar, scalar, whole, scalar],
        out_specs=vector,
        scratch_shapes=[
            pltpu.VMEM((rows, cols), BF),
            pltpu.VMEM((rows, cols), BF),
            pltpu.VMEM(shell_mask.shape, jnp.int32),
            pltpu.VMEM(table.shape, BF),
            pltpu.VMEM((bra_rows, orbitals), F32),
            pltpu.VMEM((bra_rows, orbitals), F32),
            pltpu.VMEM((ket_rows, orbitals), F32),
            pltpu.VMEM((ket_rows, orbitals), F32),
            pltpu.VMEM((512, NC * rows), BF),
            pltpu.VMEM((512, cols), F32),
            pltpu.VMEM((4, NY - 1, 32, cols), BF),
            pltpu.VMEM((4, NY - 1, 32, cols), BF),
            pltpu.VMEM((NZ - 1, OWN, cols), BF),
            pltpu.VMEM((NZ - 1, OWN, cols), BF),
            pltpu.VMEM((4, 32, cols), F32),
            pltpu.VMEM((cols, 128), F32),
            pltpu.VMEM((64, 2 * ket_rows), BF),
            pltpu.VMEM((ket_rows, 1024), F32),
            pltpu.VMEM((ket_rows, 1024), F32),
            pltpu.VMEM((NX, NY, 16, 256), F32),
            pltpu.VMEM((NY, NX, 16, 256), F32),
            pltpu.VMEM((NZ * NC, 8, 128), F32),
            pltpu.VMEM((NZ, NC, 8, 128), F32),
            dma((2,)),
            dma((2,)),
            dma((2,)),
            dma((4, NY - 1)),
            dma((4, NY - 1)),
            dma((NZ - 1,)),
            dma((NZ - 1,)),
            dma((NX * NY,)),
            dma((NX * NY,)),
            dma((NZ * NC,)),
            dma((NZ * NC,)),
        ],
        compiler_params=pltpu.CompilerParams(collective_id=0, has_side_effects=True, vmem_limit_bytes=40 * 1024 * 1024),
    )(ao_ints, shell_mask, bra_shells, ket_shells, table, mo_ranges)


def solution(mesh):
    return jax.shard_map(
        on_device,
        mesh=mesh,
        in_specs=(P("pair", "batch"), P("pair", "batch"), P(), P("batch", None), P(), P()),
        out_specs=P(("pair", "batch"), None),
        check_vma=False,
    )
```

```python
import jax
import jax.numpy as jnp
from jax import lax
from jax.experimental import pallas as pl
from jax.experimental.pallas import tpu as pltpu
from jax.sharding import PartitionSpec as P

SHELL = 8
NX, NY, NZ, NC = 4, 4, 8, 2
OWN = 16
PARTS, PART = 4, 256
LAG = 2
MESH = pl.DeviceIdType.MESH
BF = jnp.bfloat16
F32 = jnp.float32


def iota(shape, dim):
    return lax.broadcasted_iota(jnp.int32, shape, dim)


def where_one(condition):
    return jnp.where(condition, 1.0, 0.0).astype(BF)


def dot(a, b):
    return jnp.dot(a, b, preferred_element_type=F32)


def dot_last(a, b):
    return lax.dot_general(a, b, (((1,), (1,)), ((), ())), preferred_element_type=F32)


def pair_id(y, z, c):
    return (y * NZ + z) * NC + c


def kernel(
    ao_hbm, mask_ref, bra_ref, ket_ref, mo_hbm, ranges_ref, out_ref,
    ao_own, ao_other, mask_other, mo_table, bra_one, bra_two, ket_one, ket_two,
    bra_t, partial, to_y, from_y, to_z, from_z, own_sum, ket_wide, ket_narrow,
    wide_other, own_z, spread, quarter, to_xy, from_xy, to_zc, from_zc,
    load_sem, core_send, core_recv, y_send, y_recv, z_send, z_recv, xy_send, xy_recv, zc_send, zc_recv,
):
    place = lax.axis_index("pair")
    x = lax.axis_index("batch")
    c = lax.rem(place, NC)
    z = lax.rem(place // NC, NZ)
    y = place // (NC * NZ)

    def plane_peer(dx, dy):
        return (pair_id(lax.rem(y + dy, NY), z, c), lax.rem(x + dx, NX))

    def line_peer(dz, dc):
        return (pair_id(y, lax.rem(z + dz, NZ), lax.rem(c + dc, NC)), x)

    def part_of(p):
        return pl.ds(pl.multiple_of(p * PART, PART), PART)

    def load_ao(p):
        return pltpu.make_async_copy(ao_hbm.at[:, part_of(p)], ao_own.at[:, part_of(p)], load_sem.at[p])

    load_mo = pltpu.make_async_copy(mo_hbm, mo_table, load_sem.at[PARTS])
    load_mo.start()
    for p in range(PARTS):
        load_ao(p).start()
    barrier = pltpu.get_barrier_semaphore()
    plane = [(dx, dy) for dx in range(NX) for dy in range(NY) if dx or dy]
    line = [(dz, dc) for dz in range(NZ) for dc in range(NC) if dz or dc]
    for dx, dy in plane:
        pl.semaphore_signal(barrier, inc=1, device_id=plane_peer(dx, dy), device_id_type=MESH)
    for dz, dc in line:
        pl.semaphore_signal(barrier, inc=1, device_id=line_peer(dz, dc), device_id_type=MESH)

    load_mo.wait()
    half = mask_ref.shape[0]
    first_pair = place * half
    other_pair = pair_id(y, z, lax.rem(c + 1, NC)) * half

    def take_bra(t, carry):
        spot = pl.ds(pl.multiple_of(t * SHELL, SHELL), SHELL)
        late = pl.ds(pl.multiple_of((half + t) * SHELL, SHELL), SHELL)
        bra_one[spot, :] = mo_table[bra_ref[0, first_pair + t]].astype(F32)
        bra_two[spot, :] = mo_table[bra_ref[1, first_pair + t]].astype(F32)
        bra_one[late, :] = mo_table[bra_ref[0, other_pair + t]].astype(F32)
        bra_two[late, :] = mo_table[bra_ref[1, other_pair + t]].astype(F32)
        return carry

    lax.fori_loop(0, half, take_bra, 0)

    def take_ket(s, carry):
        spot = pl.ds(pl.multiple_of(s * SHELL, SHELL), SHELL)
        ket_one[spot, :] = mo_table[ket_ref[0, s]].astype(F32)
        ket_two[spot, :] = mo_table[ket_ref[1, s]].astype(F32)
        return carry

    lax.fori_loop(0, ket_ref.shape[1], take_ket, 0)

    pl.semaphore_wait(barrier, len(plane) + len(line))

    def ao_copy(p):
        return pltpu.make_async_remote_copy(
            ao_hbm.at[:, part_of(p)], ao_other.at[:, part_of(p)], core_send.at[p], core_recv.at[p],
            device_id=line_peer(0, 1), device_id_type=MESH,
        )

    mask_copy = pltpu.make_async_remote_copy(
        mask_ref, mask_other, core_send.at[PARTS], core_recv.at[PARTS], device_id=line_peer(0, 1), device_id_type=MESH
    )
    mask_copy.start()
    for p in range(PARTS):
        ao_copy(p).start()

    depth = bra_one.shape[0]
    width = bra_t.shape[1]
    orbitals = bra_one.shape[1]
    row = iota((bra_t.shape[0], orbitals), 0)
    to_z_place = (z + ((row >> 4) & 7)) & (NZ - 1)
    to_y_place = (y + (row >> 7)) & (NY - 1)
    ab = to_z_place * 128 + c * 64 + to_y_place * 16 + (row & 15)
    orbital = iota((bra_t.shape[0], orbitals), 1)
    pick_a = where_one(orbital == ranges_ref[2] + (ab >> 5))
    pick_b = where_one(orbital == ranges_ref[3] + (ab & 31))
    small_a = dot_last(pick_a, bra_one[...].astype(BF)).astype(BF)
    small_b = dot_last(pick_b, bra_two[...].astype(BF)).astype(BF)
    source = iota((depth, width), 0)
    column = iota((depth, width), 1)
    over_m = where_one(source == (column >> 3))
    over_n = where_one(((source >> 3) == (column >> 6)) & ((source & 7) == (column & 7)))
    for start in range(0, bra_t.shape[0], 128):
        rows = slice(start, start + 128)
        bra_t[rows, :] = (dot(small_a[rows], over_m) * dot(small_b[rows], over_n)).astype(BF)

    mask_spread = where_one(
        iota((mask_ref.shape[1], ao_own.shape[1]), 0) == (iota((mask_ref.shape[1], ao_own.shape[1]), 1) >> 6)
    )

    own_wide = dot(mask_ref[...].astype(F32).astype(BF), mask_spread)
    wide_other[0] = own_wide

    def screen(values, wide, p):
        factor = wide[:, part_of(p)].astype(BF)
        for t in range(half):
            block = slice(64 * t, 64 * t + 64)
            values[block, part_of(p)] = values[block, part_of(p)] * factor[t:t + 1, :]

    own_width = ao_own.shape[0]

    def own_part(p, carry):
        load_ao(p).wait()
        screen(ao_own, wide_other.at[0], p)
        for dy in range(NY):
            rows = slice(128 * dy, 128 * dy + 128)
            partial[rows, part_of(p)] = dot(bra_t[rows, :own_width], ao_own[:, part_of(p)])
        return carry

    lax.fori_loop(0, PARTS, own_part, 0)
    mask_copy.wait_recv()
    wide_other[1] = dot(mask_other[...].astype(F32).astype(BF), mask_spread)

    def y_copy(p, dy):
        return pltpu.make_async_remote_copy(
            to_y.at[p, dy - 1], from_y.at[p, dy - 1], y_send.at[p, dy - 1], y_recv.at[p, dy - 1],
            device_id=plane_peer(0, dy), device_id_type=MESH,
        )

    def other_part(p, carry):
        ao_copy(p).wait_recv()
        screen(ao_other, wide_other.at[1], p)
        for dy in (2, 1, 3, 0):
            rows = slice(128 * dy, 128 * dy + 128)
            total = partial[rows, part_of(p)] + dot(bra_t[rows, own_width:], ao_other[:, part_of(p)])
            if dy:
                to_y[p, dy - 1] = total.astype(BF)
                y_copy(p, dy).start()
            else:
                own_sum[p] = total
        return carry

    lax.fori_loop(0, PARTS, other_part, 0)

    columns = spread.shape[1]
    col = iota((orbitals, columns), 1)
    first = (((y + (col >> 8)) & (NY - 1)) << 4) + (((z + ((col >> 5) & 7)) & (NZ - 1)) << 1) + ((c + (col >> 4)) & 1)
    pick_i = where_one(iota((orbitals, columns), 0) == ranges_ref[0] + first)
    spread[...] = dot(ket_one[...].astype(BF), pick_i)
    j_row = iota((ket_narrow.shape[0], orbitals), 0)
    second = (((x + (j_row >> 4)) & (NX - 1)) << 4) + (j_row & 15)
    pick_j = where_one(iota((ket_narrow.shape[0], orbitals), 1) == ranges_ref[1] + second)
    narrow = dot_last(pick_j, ket_two[...].astype(BF)).astype(BF)
    ket_narrow[...] = jnp.concatenate([narrow, narrow], axis=1)

    def z_copy(p, dz):
        return pltpu.make_async_remote_copy(
            to_z.at[p, dz - 1], from_z.at[p, dz - 1], z_send.at[p, dz - 1], z_recv.at[p, dz - 1],
            device_id=line_peer(dz, 0), device_id_type=MESH,
        )

    def over_y(p):
        for dy in range(1, NY):
            y_copy(p, dy).wait_recv()
        for dz in (4, 3, 5, 2, 6, 1, 7, 0):
            rows = slice(OWN * dz, OWN * dz + OWN)
            part = own_sum[p, rows]
            for dy in range(1, NY):
                part = part + from_y[p, dy - 1, rows].astype(F32)
            if dz:
                to_z[p, dz - 1] = part.astype(BF)
                z_copy(p, dz).start()
            else:
                own_z[p] = part

    lanes = where_one((iota((2 * OWN, 128), 0) & 15) == (iota((2 * OWN, 128), 1) & 15))

    def over_first(s, carry):
        sums = [None] * (columns // 128)
        factors = spread[pl.ds(pl.multiple_of(s * SHELL, SHELL), SHELL), :]
        for m in range(SHELL):
            block = ket_wide[pl.ds(pl.multiple_of((s * SHELL + m) * SHELL, SHELL), SHELL), :]
            for tile in range(columns // 128):
                term = factors[m:m + 1, 128 * tile:128 * tile + 128] * block
                sums[tile] = term if m == 0 else sums[tile] + term
        for tile in range(columns // 128):
            quarter[pl.ds(pl.multiple_of(s * SHELL, SHELL), SHELL), 128 * tile:128 * tile + 128] = sums[tile]
        return carry

    pairs = PART // (SHELL * SHELL)

    def over_z(p):
        summed = own_z[p]
        for dz in (1, 7, 2, 6, 3, 5, 4):
            z_copy(p, dz).wait_recv()
            summed = summed + from_z[p, dz - 1].astype(F32)
        high = summed.astype(BF)
        low = (summed - high.astype(F32)).astype(BF)
        ket_wide[part_of(p), :] = lax.dot_general(
            jnp.concatenate([high, low], axis=0), lanes, (((0,), (0,)), ((), ())), preferred_element_type=F32
        )
        lax.fori_loop(p * pairs, p * pairs + pairs, over_first, 0)

    def step(p, carry):
        over_y(p)
        return carry

    def both_steps(p, carry):
        over_y(p)
        over_z(p - LAG)
        return carry

    def last_step(p, carry):
        over_z(p)
        return carry

    lax.fori_loop(0, LAG, step, 0)
    lax.fori_loop(LAG, PARTS, both_steps, 0)
    lax.fori_loop(PARTS - LAG, PARTS, last_step, 0)
    value = quarter[...]
    value_high = value.astype(BF)
    value_low = (value - value_high.astype(F32)).astype(BF)
    both = dot(ket_narrow[...], jnp.concatenate([value_high, value_low], axis=0))

    def plane_copy(dx, dy, slot):
        return pltpu.make_async_remote_copy(
            to_xy.at[dx, dy], from_xy.at[slot[0], slot[1]], xy_send.at[dx * NY + dy], xy_recv.at[dx * NY + dy],
            device_id=plane_peer(dx, dy), device_id_type=MESH,
        )

    for dx, dy in sorted(plane, key=lambda d: -min(d[0], NX - d[0]) - min(d[1], NY - d[1])):
        to_xy[dx, dy] = both[16 * dx:16 * dx + 16, 256 * dy:256 * dy + 256]
        plane_copy(dx, dy, (y, x)).start()
    from_xy[y, x] = both[:16, :256]
    for dx, dy in plane:
        plane_copy(dx, dy, (lax.rem(y + NY - dy, NY), lax.rem(x + NX - dx, NX))).wait_recv()
    merged = [from_xy[k, 0] + from_xy[k, 1] + from_xy[k, 2] + from_xy[k, 3] for k in range(NY)]

    def line_copy(dz, dc, slot):
        return pltpu.make_async_remote_copy(
            to_zc.at[dz * NC + dc], from_zc.at[slot[0], slot[1]], zc_send.at[dz * NC + dc], zc_recv.at[dz * NC + dc],
            device_id=line_peer(dz, dc), device_id_type=MESH,
        )

    lane = iota((8, 128), 1)
    for dz, dc in sorted([(dz, dc) for dz in range(NZ) for dc in range(NC)], key=lambda d: -min(d[0], NZ - d[0])):
        group = dz * NC + dc
        tile = slice(128 * (group // 8), 128 * (group // 8) + 128)
        message = None
        for k in range(8):
            block = merged[k % 4][8 * (k // 4):8 * (k // 4) + 8, tile]
            shift = (16 * k - 16 * (group % 8)) % 128
            moved = pltpu.roll(block, shift, 1) if shift else block
            message = moved if message is None else jnp.where((lane >> 4) == k, moved, message)
        if group:
            to_zc[group] = message
            line_copy(dz, dc, (z, c)).start()
        else:
            from_zc[z, c] = message
    for dz, dc in line:
        line_copy(dz, dc, (lax.rem(z + NZ - dz, NZ), lax.rem(c + NC - dc, NC))).wait_recv()
    for k in range(NZ):
        left, right = from_zc[k, 0], from_zc[k, 1]
        out_ref[0:8, 128 * k:128 * k + 128] = jnp.where(lane < 64, left, pltpu.roll(right, 64, 1))
        out_ref[8:16, 128 * k:128 * k + 128] = jnp.where(lane < 64, pltpu.roll(left, 64, 1), right)

    mask_copy.wait_send()

    def drain(p, carry):
        ao_copy(p).wait_send()
        for dy in range(1, NY):
            y_copy(p, dy).wait_send()
        for dz in range(1, NZ):
            z_copy(p, dz).wait_send()
        return carry

    lax.fori_loop(0, PARTS, drain, 0)
    for dx, dy in plane:
        plane_copy(dx, dy, (y, x)).wait_send()
    for dz, dc in line:
        line_copy(dz, dc, (z, c)).wait_send()


def on_device(ao_ints, shell_mask, bra_shells, ket_shells, mo_coeff, mo_ranges):
    table = mo_coeff.reshape(mo_coeff.shape[0] // SHELL, SHELL, mo_coeff.shape[1])
    rows, cols = ao_ints.shape
    orbitals = mo_coeff.shape[1]
    ket_rows = ket_shells.shape[0] * SHELL
    bra_rows = NC * shell_mask.shape[0] * SHELL
    dma = pltpu.SemaphoreType.DMA
    whole = pl.BlockSpec(memory_space=pltpu.HBM)
    scalar = pl.BlockSpec(memory_space=pltpu.SMEM)
    vector = pl.BlockSpec(memory_space=pltpu.VMEM)
    return pl.pallas_call(
        kernel,
        out_shape=jax.ShapeDtypeStruct((16, 1024), F32),
        in_specs=[whole, vector, scalar, scalar, whole, scalar],
        out_specs=vector,
        scratch_shapes=[
            pltpu.VMEM((rows, cols), BF),
            pltpu.VMEM((rows, cols), BF),
            pltpu.VMEM(shell_mask.shape, jnp.int32),
            pltpu.VMEM(table.shape, BF),
            pltpu.VMEM((bra_rows, orbitals), F32),
            pltpu.VMEM((bra_rows, orbitals), F32),
            pltpu.VMEM((ket_rows, orbitals), F32),
            pltpu.VMEM((ket_rows, orbitals), F32),
            pltpu.VMEM((512, NC * rows), BF),
            pltpu.VMEM((512, cols), F32),
            pltpu.VMEM((PARTS, NY - 1, NZ * OWN, PART), BF),
            pltpu.VMEM((PARTS, NY - 1, NZ * OWN, PART), BF),
            pltpu.VMEM((PARTS, NZ - 1, OWN, PART), BF),
            pltpu.VMEM((PARTS, NZ - 1, OWN, PART), BF),
            pltpu.VMEM((PARTS, NZ * OWN, PART), F32),
            pltpu.VMEM((cols, 128), F32),
            pltpu.VMEM((64, 2 * ket_rows), BF),
            pltpu.VMEM((NC, shell_mask.shape[0], cols), F32),
            pltpu.VMEM((PARTS, OWN, PART), F32),
            pltpu.VMEM((ket_rows, 1024), F32),
            pltpu.VMEM((ket_rows, 1024), F32),
            pltpu.VMEM((NX, NY, 16, 256), F32),
            pltpu.VMEM((NY, NX, 16, 256), F32),
            pltpu.VMEM((NZ * NC, 8, 128), F32),
            pltpu.VMEM((NZ, NC, 8, 128), F32),
            dma((PARTS + 1,)),
            dma((PARTS + 1,)),
            dma((PARTS + 1,)),
            dma((PARTS, NY - 1)),
            dma((PARTS, NY - 1)),
            dma((PARTS, NZ - 1)),
            dma((PARTS, NZ - 1)),
            dma((NX * NY,)),
            dma((NX * NY,)),
            dma((NZ * NC,)),
            dma((NZ * NC,)),
        ],
        compiler_params=pltpu.CompilerParams(collective_id=0, has_side_effects=True, vmem_limit_bytes=67_043_328),
    )(ao_ints, shell_mask, bra_shells.T, ket_shells.T, table, mo_ranges)


def solution(mesh):
    return jax.shard_map(
        on_device,
        mesh=mesh,
        in_specs=(P("pair", "batch"), P("pair", "batch"), P(), P("batch", None), P(), P()),
        out_specs=P(("pair", "batch"), None),
        check_vma=False,
    )
```

```python
import jax
import jax.numpy as jnp
from jax import lax
from jax.experimental import pallas as pl
from jax.experimental.pallas import tpu as pltpu
from jax.sharding import PartitionSpec as P

SHELL = 8
NX, NY, NZ, NC = 4, 4, 8, 2
OWN = 16
PARTS, PART = 4, 256
LAG = 2
MESH = pl.DeviceIdType.MESH
BF = jnp.bfloat16
F32 = jnp.float32


def iota(shape, dim):
    return lax.broadcasted_iota(jnp.int32, shape, dim)


def where_one(condition):
    return jnp.where(condition, 1.0, 0.0).astype(BF)


def dot(a, b):
    return jnp.dot(a, b, preferred_element_type=F32)


def dot_last(a, b):
    return lax.dot_general(a, b, (((1,), (1,)), ((), ())), preferred_element_type=F32)


def pair_id(y, z, c):
    return (y * NZ + z) * NC + c


def kernel(
    ao_hbm, mask_ref, bra_ref, ket_ref, mo_hbm, ranges_ref, out_ref,
    ao_own, ao_other, mask_other, mo_table, bra_one, bra_two, ket_one, ket_two,
    bra_t, partial, to_y, from_y, to_z, from_z, own_sum, ket_wide, ket_narrow,
    wide_other, own_z, to_relay, from_relay, kept, spread, quarter, to_xy, from_xy, to_zc, from_zc,
    load_sem, core_send, core_recv, y_send, y_recv, relay_send, relay_recv, z_send, z_recv, xy_send, xy_recv, zc_send, zc_recv,
):
    place = lax.axis_index("pair")
    x = lax.axis_index("batch")
    c = lax.rem(place, NC)
    z = lax.rem(place // NC, NZ)
    y = place // (NC * NZ)

    def plane_peer(dx, dy):
        return (pair_id(lax.rem(y + dy, NY), z, c), lax.rem(x + dx, NX))

    def line_peer(dz, dc):
        return (pair_id(y, lax.rem(z + dz, NZ), lax.rem(c + dc, NC)), x)

    def part_of(p):
        return pl.ds(pl.multiple_of(p * PART, PART), PART)

    def load_ao(p):
        return pltpu.make_async_copy(ao_hbm.at[:, part_of(p)], ao_own.at[:, part_of(p)], load_sem.at[p])

    load_mo = pltpu.make_async_copy(mo_hbm, mo_table, load_sem.at[PARTS])
    load_mo.start()
    for p in range(PARTS):
        load_ao(p).start()
    barrier = pltpu.get_barrier_semaphore()
    plane = [(dx, dy) for dx in range(NX) for dy in range(NY) if dx or dy]
    line = [(dz, dc) for dz in range(NZ) for dc in range(NC) if dz or dc]
    for dx, dy in plane:
        pl.semaphore_signal(barrier, inc=1, device_id=plane_peer(dx, dy), device_id_type=MESH)
    for dz, dc in line:
        pl.semaphore_signal(barrier, inc=1, device_id=line_peer(dz, dc), device_id_type=MESH)

    load_mo.wait()
    half = mask_ref.shape[0]
    first_pair = place * half
    other_pair = pair_id(y, z, lax.rem(c + 1, NC)) * half

    def take_bra(t, carry):
        spot = pl.ds(pl.multiple_of(t * SHELL, SHELL), SHELL)
        late = pl.ds(pl.multiple_of((half + t) * SHELL, SHELL), SHELL)
        bra_one[spot, :] = mo_table[bra_ref[0, first_pair + t]].astype(F32)
        bra_two[spot, :] = mo_table[bra_ref[1, first_pair + t]].astype(F32)
        bra_one[late, :] = mo_table[bra_ref[0, other_pair + t]].astype(F32)
        bra_two[late, :] = mo_table[bra_ref[1, other_pair + t]].astype(F32)
        return carry

    lax.fori_loop(0, half, take_bra, 0)

    def take_ket(s, carry):
        spot = pl.ds(pl.multiple_of(s * SHELL, SHELL), SHELL)
        ket_one[spot, :] = mo_table[ket_ref[0, s]].astype(F32)
        ket_two[spot, :] = mo_table[ket_ref[1, s]].astype(F32)
        return carry

    lax.fori_loop(0, ket_ref.shape[1], take_ket, 0)

    pl.semaphore_wait(barrier, len(plane) + len(line))

    def ao_copy(p):
        return pltpu.make_async_remote_copy(
            ao_hbm.at[:, part_of(p)], ao_other.at[:, part_of(p)], core_send.at[p], core_recv.at[p],
            device_id=line_peer(0, 1), device_id_type=MESH,
        )

    mask_copy = pltpu.make_async_remote_copy(
        mask_ref, mask_other, core_send.at[PARTS], core_recv.at[PARTS], device_id=line_peer(0, 1), device_id_type=MESH
    )
    mask_copy.start()
    for p in range(PARTS):
        ao_copy(p).start()

    depth = bra_one.shape[0]
    width = bra_t.shape[1]
    orbitals = bra_one.shape[1]
    row = iota((bra_t.shape[0], orbitals), 0)
    to_z_place = (z + ((row >> 4) & 7)) & (NZ - 1)
    to_y_place = (y + (row >> 7)) & (NY - 1)
    ab = to_z_place * 128 + c * 64 + to_y_place * 16 + (row & 15)
    orbital = iota((bra_t.shape[0], orbitals), 1)
    pick_a = where_one(orbital == ranges_ref[2] + (ab >> 5))
    pick_b = where_one(orbital == ranges_ref[3] + (ab & 31))
    small_a = dot_last(pick_a, bra_one[...].astype(BF)).astype(BF)
    small_b = dot_last(pick_b, bra_two[...].astype(BF)).astype(BF)
    source = iota((depth, width), 0)
    column = iota((depth, width), 1)
    over_m = where_one(source == (column >> 3))
    over_n = where_one(((source >> 3) == (column >> 6)) & ((source & 7) == (column & 7)))
    for start in range(0, bra_t.shape[0], 128):
        rows = slice(start, start + 128)
        bra_t[rows, :] = (dot(small_a[rows], over_m) * dot(small_b[rows], over_n)).astype(BF)

    mask_spread = where_one(
        iota((mask_ref.shape[1], ao_own.shape[1]), 0) == (iota((mask_ref.shape[1], ao_own.shape[1]), 1) >> 6)
    )

    own_wide = dot(mask_ref[...].astype(F32).astype(BF), mask_spread)
    wide_other[0] = own_wide

    def screen(values, wide, p):
        factor = wide[:, part_of(p)].astype(BF)
        for t in range(half):
            block = slice(64 * t, 64 * t + 64)
            values[block, part_of(p)] = values[block, part_of(p)] * factor[t:t + 1, :]

    own_width = ao_own.shape[0]

    def own_part(p, carry):
        load_ao(p).wait()
        screen(ao_own, wide_other.at[0], p)
        for dy in range(NY):
            rows = slice(128 * dy, 128 * dy + 128)
            partial[rows, part_of(p)] = dot(bra_t[rows, :own_width], ao_own[:, part_of(p)])
        return carry

    lax.fori_loop(0, PARTS, own_part, 0)
    mask_copy.wait_recv()
    wide_other[1] = dot(mask_other[...].astype(F32).astype(BF), mask_spread)

    ways = (1, NY - 1)
    rows_y = NZ * OWN
    half_rows = (slice(0, rows_y // 2), slice(rows_y // 2, rows_y))

    def y_copy(p, way, part):
        return pltpu.make_async_remote_copy(
            to_y.at[p, way, part], from_y.at[p, way, part], y_send.at[p, way, part], y_recv.at[p, way, part],
            device_id=plane_peer(0, ways[way]), device_id_type=MESH,
        )

    def relay_copy(p, way):
        return pltpu.make_async_remote_copy(
            to_relay.at[p, way], from_relay.at[p, way], relay_send.at[p, way], relay_recv.at[p, way],
            device_id=plane_peer(0, ways[way]), device_id_type=MESH,
        )

    def other_part(p, carry):
        ao_copy(p).wait_recv()
        screen(ao_other, wide_other.at[1], p)
        for dy in (2, 1, 3, 0):
            rows = slice(rows_y * dy, rows_y * dy + rows_y)
            total = partial[rows, part_of(p)] + dot(bra_t[rows, own_width:], ao_other[:, part_of(p)])
            if dy == 0:
                own_sum[p] = total
            elif dy == 2:
                for way in range(2):
                    to_relay[p, way] = total[half_rows[way]].astype(BF)
                    relay_copy(p, way).start()
            else:
                way = ways.index(dy)
                kept[p, way] = total[half_rows[way]]
                to_y[p, way, 1 - way] = total[half_rows[1 - way]].astype(BF)
                y_copy(p, way, 1 - way).start()
        return carry

    def relay(p, carry):
        for way in range(2):
            relay_copy(p, way).wait_recv()
            to_y[p, way, way] = (kept[p, way] + from_relay[p, way].astype(F32)).astype(BF)
            y_copy(p, way, way).start()
        return carry

    def other_and_relay(p, carry):
        return relay(p - LAG, other_part(p, carry))

    lax.fori_loop(0, LAG, other_part, 0)
    lax.fori_loop(LAG, PARTS, other_and_relay, 0)

    columns = spread.shape[1]
    col = iota((orbitals, columns), 1)
    first = (((y + (col >> 8)) & (NY - 1)) << 4) + (((z + ((col >> 5) & 7)) & (NZ - 1)) << 1) + ((c + (col >> 4)) & 1)
    pick_i = where_one(iota((orbitals, columns), 0) == ranges_ref[0] + first)
    spread[...] = dot(ket_one[...].astype(BF), pick_i)
    j_row = iota((ket_narrow.shape[0], orbitals), 0)
    second = (((x + (j_row >> 4)) & (NX - 1)) << 4) + (j_row & 15)
    pick_j = where_one(iota((ket_narrow.shape[0], orbitals), 1) == ranges_ref[1] + second)
    narrow = dot_last(pick_j, ket_two[...].astype(BF)).astype(BF)
    ket_narrow[...] = jnp.concatenate([narrow, narrow], axis=1)

    def z_copy(p, dz):
        return pltpu.make_async_remote_copy(
            to_z.at[p, dz - 1], from_z.at[p, dz - 1], z_send.at[p, dz - 1], z_recv.at[p, dz - 1],
            device_id=line_peer(dz, 0), device_id_type=MESH,
        )

    def over_y(p):
        for way in range(2):
            for part in (1 - way, way):
                y_copy(p, way, part).wait_recv()
        for dz in (4, 3, 5, 2, 6, 1, 7, 0):
            part = own_sum[p, OWN * dz:OWN * dz + OWN]
            start = OWN * dz % (rows_y // 2)
            for way in range(2):
                part = part + from_y[p, way, 2 * dz // NZ, start:start + OWN].astype(F32)
            if dz:
                to_z[p, dz - 1] = part.astype(BF)
                z_copy(p, dz).start()
            else:
                own_z[p] = part

    lanes = where_one((iota((2 * OWN, 128), 0) & 15) == (iota((2 * OWN, 128), 1) & 15))

    def over_first(s, carry):
        sums = [None] * (columns // 128)
        factors = spread[pl.ds(pl.multiple_of(s * SHELL, SHELL), SHELL), :]
        for m in range(SHELL):
            block = ket_wide[pl.ds(pl.multiple_of((s * SHELL + m) * SHELL, SHELL), SHELL), :]
            for tile in range(columns // 128):
                term = factors[m:m + 1, 128 * tile:128 * tile + 128] * block
                sums[tile] = term if m == 0 else sums[tile] + term
        for tile in range(columns // 128):
            quarter[pl.ds(pl.multiple_of(s * SHELL, SHELL), SHELL), 128 * tile:128 * tile + 128] = sums[tile]
        return carry

    pairs = PART // (SHELL * SHELL)

    def over_z(p):
        summed = own_z[p]
        for dz in (1, 7, 2, 6, 3, 5, 4):
            z_copy(p, dz).wait_recv()
            summed = summed + from_z[p, dz - 1].astype(F32)
        high = summed.astype(BF)
        low = (summed - high.astype(F32)).astype(BF)
        ket_wide[part_of(p), :] = lax.dot_general(
            jnp.concatenate([high, low], axis=0), lanes, (((0,), (0,)), ((), ())), preferred_element_type=F32
        )
        lax.fori_loop(p * pairs, p * pairs + pairs, over_first, 0)

    def step(p, carry):
        relay(p + PARTS - LAG, 0)
        over_y(p)
        return carry

    def both_steps(p, carry):
        over_y(p)
        over_z(p - LAG)
        return carry

    def last_step(p, carry):
        over_z(p)
        return carry

    lax.fori_loop(0, LAG, step, 0)
    lax.fori_loop(LAG, PARTS, both_steps, 0)
    lax.fori_loop(PARTS - LAG, PARTS, last_step, 0)
    value = quarter[...]
    value_high = value.astype(BF)
    value_low = (value - value_high.astype(F32)).astype(BF)
    both = dot(ket_narrow[...], jnp.concatenate([value_high, value_low], axis=0))

    def plane_copy(dx, dy, slot):
        return pltpu.make_async_remote_copy(
            to_xy.at[dx, dy], from_xy.at[slot[0], slot[1]], xy_send.at[dx * NY + dy], xy_recv.at[dx * NY + dy],
            device_id=plane_peer(dx, dy), device_id_type=MESH,
        )

    for dx, dy in sorted(plane, key=lambda d: -min(d[0], NX - d[0]) - min(d[1], NY - d[1])):
        to_xy[dx, dy] = both[16 * dx:16 * dx + 16, 256 * dy:256 * dy + 256]
        plane_copy(dx, dy, (y, x)).start()
    from_xy[y, x] = both[:16, :256]
    for dx, dy in plane:
        plane_copy(dx, dy, (lax.rem(y + NY - dy, NY), lax.rem(x + NX - dx, NX))).wait_recv()
    merged = [from_xy[k, 0] + from_xy[k, 1] + from_xy[k, 2] + from_xy[k, 3] for k in range(NY)]

    def line_copy(dz, dc, slot):
        return pltpu.make_async_remote_copy(
            to_zc.at[dz * NC + dc], from_zc.at[slot[0], slot[1]], zc_send.at[dz * NC + dc], zc_recv.at[dz * NC + dc],
            device_id=line_peer(dz, dc), device_id_type=MESH,
        )

    lane = iota((8, 128), 1)
    for dz, dc in sorted([(dz, dc) for dz in range(NZ) for dc in range(NC)], key=lambda d: -min(d[0], NZ - d[0])):
        group = dz * NC + dc
        tile = slice(128 * (group // 8), 128 * (group // 8) + 128)
        message = None
        for k in range(8):
            block = merged[k % 4][8 * (k // 4):8 * (k // 4) + 8, tile]
            shift = (16 * k - 16 * (group % 8)) % 128
            moved = pltpu.roll(block, shift, 1) if shift else block
            message = moved if message is None else jnp.where((lane >> 4) == k, moved, message)
        if group:
            to_zc[group] = message
            line_copy(dz, dc, (z, c)).start()
        else:
            from_zc[z, c] = message
    for dz, dc in line:
        line_copy(dz, dc, (lax.rem(z + NZ - dz, NZ), lax.rem(c + NC - dc, NC))).wait_recv()
    for k in range(NZ):
        left, right = from_zc[k, 0], from_zc[k, 1]
        out_ref[0:8, 128 * k:128 * k + 128] = jnp.where(lane < 64, left, pltpu.roll(right, 64, 1))
        out_ref[8:16, 128 * k:128 * k + 128] = jnp.where(lane < 64, pltpu.roll(left, 64, 1), right)

    mask_copy.wait_send()

    def drain(p, carry):
        ao_copy(p).wait_send()
        for way in range(2):
            relay_copy(p, way).wait_send()
            y_copy(p, way, 0).wait_send()
            y_copy(p, way, 1).wait_send()
        for dz in range(1, NZ):
            z_copy(p, dz).wait_send()
        return carry

    lax.fori_loop(0, PARTS, drain, 0)
    for dx, dy in plane:
        plane_copy(dx, dy, (y, x)).wait_send()
    for dz, dc in line:
        line_copy(dz, dc, (z, c)).wait_send()


def on_device(ao_ints, shell_mask, bra_shells, ket_shells, mo_coeff, mo_ranges):
    table = mo_coeff.reshape(mo_coeff.shape[0] // SHELL, SHELL, mo_coeff.shape[1])
    rows, cols = ao_ints.shape
    orbitals = mo_coeff.shape[1]
    ket_rows = ket_shells.shape[0] * SHELL
    bra_rows = NC * shell_mask.shape[0] * SHELL
    dma = pltpu.SemaphoreType.DMA
    whole = pl.BlockSpec(memory_space=pltpu.HBM)
    scalar = pl.BlockSpec(memory_space=pltpu.SMEM)
    vector = pl.BlockSpec(memory_space=pltpu.VMEM)
    return pl.pallas_call(
        kernel,
        out_shape=jax.ShapeDtypeStruct((16, 1024), F32),
        in_specs=[whole, vector, scalar, scalar, whole, scalar],
        out_specs=vector,
        scratch_shapes=[
            pltpu.VMEM((rows, cols), BF),
            pltpu.VMEM((rows, cols), BF),
            pltpu.VMEM(shell_mask.shape, jnp.int32),
            pltpu.VMEM(table.shape, BF),
            pltpu.VMEM((bra_rows, orbitals), F32),
            pltpu.VMEM((bra_rows, orbitals), F32),
            pltpu.VMEM((ket_rows, orbitals), F32),
            pltpu.VMEM((ket_rows, orbitals), F32),
            pltpu.VMEM((512, NC * rows), BF),
            pltpu.VMEM((512, cols), F32),
            pltpu.VMEM((PARTS, 2, 2, NZ * OWN // 2, PART), BF),
            pltpu.VMEM((PARTS, 2, 2, NZ * OWN // 2, PART), BF),
            pltpu.VMEM((PARTS, NZ - 1, OWN, PART), BF),
            pltpu.VMEM((PARTS, NZ - 1, OWN, PART), BF),
            pltpu.VMEM((PARTS, NZ * OWN, PART), F32),
            pltpu.VMEM((cols, 128), F32),
            pltpu.VMEM((64, 2 * ket_rows), BF),
            pltpu.VMEM((NC, shell_mask.shape[0], cols), F32),
            pltpu.VMEM((PARTS, OWN, PART), F32),
            pltpu.VMEM((PARTS, 2, NZ * OWN // 2, PART), BF),
            pltpu.VMEM((PARTS, 2, NZ * OWN // 2, PART), BF),
            pltpu.VMEM((PARTS, 2, NZ * OWN // 2, PART), F32),
            pltpu.VMEM((ket_rows, 1024), F32),
            pltpu.VMEM((ket_rows, 1024), F32),
            pltpu.VMEM((NX, NY, 16, 256), F32),
            pltpu.VMEM((NY, NX, 16, 256), F32),
            pltpu.VMEM((NZ * NC, 8, 128), F32),
            pltpu.VMEM((NZ, NC, 8, 128), F32),
            dma((PARTS + 1,)),
            dma((PARTS + 1,)),
            dma((PARTS + 1,)),
            dma((PARTS, 2, 2)),
            dma((PARTS, 2, 2)),
            dma((PARTS, 2)),
            dma((PARTS, 2)),
            dma((PARTS, NZ - 1)),
            dma((PARTS, NZ - 1)),
            dma((NX * NY,)),
            dma((NX * NY,)),
            dma((NZ * NC,)),
            dma((NZ * NC,)),
        ],
        compiler_params=pltpu.CompilerParams(collective_id=0, has_side_effects=True, vmem_limit_bytes=67_043_328),
    )(ao_ints, shell_mask, bra_shells.T, ket_shells.T, table, mo_ranges)


def solution(mesh):
    return jax.shard_map(
        on_device,
        mesh=mesh,
        in_specs=(P("pair", "batch"), P("pair", "batch"), P(), P("batch", None), P(), P()),
        out_specs=P(("pair", "batch"), None),
        check_vma=False,
    )
```

```python
import jax
import jax.numpy as jnp
from jax import lax
from jax.experimental import pallas as pl
from jax.experimental.pallas import tpu as pltpu
from jax.sharding import PartitionSpec as P

SHELL = 8
NX, NY, NZ, NC = 4, 4, 8, 2
OWN = 16
PARTS, PART = 4, 256
LAG = 2
MESH = pl.DeviceIdType.MESH
BF = jnp.bfloat16
F32 = jnp.float32


def iota(shape, dim):
    return lax.broadcasted_iota(jnp.int32, shape, dim)


def where_one(condition):
    return jnp.where(condition, 1.0, 0.0).astype(BF)


def dot(a, b):
    return jnp.dot(a, b, preferred_element_type=F32)


def dot_last(a, b):
    return lax.dot_general(a, b, (((1,), (1,)), ((), ())), preferred_element_type=F32)


def pair_id(y, z, c):
    return (y * NZ + z) * NC + c


def kernel(
    ao_hbm, mask_ref, bra_ref, ket_ref, mo_hbm, ranges_ref, out_ref,
    ao_own, ao_other, mask_other, mo_table, bra_one, bra_two, ket_one, ket_two,
    bra_t, partial, to_y, from_y, to_z, from_z, own_sum, ket_wide, ket_narrow,
    wide_other, own_z, to_relay, from_relay, kept, spread, quarter, to_xy, from_xy, to_zc, from_zc,
    load_sem, core_send, core_recv, y_send, y_recv, relay_send, relay_recv, z_send, z_recv, xy_send, xy_recv, zc_send, zc_recv,
):
    place = lax.axis_index("pair")
    x = lax.axis_index("batch")
    c = lax.rem(place, NC)
    z = lax.rem(place // NC, NZ)
    y = place // (NC * NZ)

    def plane_peer(dx, dy):
        return (pair_id(lax.rem(y + dy, NY), z, c), lax.rem(x + dx, NX))

    def line_peer(dz, dc):
        return (pair_id(y, lax.rem(z + dz, NZ), lax.rem(c + dc, NC)), x)

    def part_of(p):
        return pl.ds(pl.multiple_of(p * PART, PART), PART)

    def load_ao(p):
        return pltpu.make_async_copy(ao_hbm.at[:, part_of(p)], ao_own.at[:, part_of(p)], load_sem.at[p])

    load_mo = pltpu.make_async_copy(mo_hbm, mo_table, load_sem.at[PARTS])
    load_mo.start()
    for p in range(PARTS):
        load_ao(p).start()
    barrier = pltpu.get_barrier_semaphore()
    plane = [(dx, dy) for dx in range(NX) for dy in range(NY) if dx or dy]
    line = [(dz, dc) for dz in range(NZ) for dc in range(NC) if dz or dc]
    for dx, dy in plane:
        pl.semaphore_signal(barrier, inc=1, device_id=plane_peer(dx, dy), device_id_type=MESH)
    for dz, dc in line:
        pl.semaphore_signal(barrier, inc=1, device_id=line_peer(dz, dc), device_id_type=MESH)

    load_mo.wait()
    half = mask_ref.shape[0]
    first_pair = place * half
    other_pair = pair_id(y, z, lax.rem(c + 1, NC)) * half

    def take_bra(t, carry):
        spot = pl.ds(pl.multiple_of(t * SHELL, SHELL), SHELL)
        late = pl.ds(pl.multiple_of((half + t) * SHELL, SHELL), SHELL)
        bra_one[spot, :] = mo_table[bra_ref[0, first_pair + t]].astype(F32)
        bra_two[spot, :] = mo_table[bra_ref[1, first_pair + t]].astype(F32)
        bra_one[late, :] = mo_table[bra_ref[0, other_pair + t]].astype(F32)
        bra_two[late, :] = mo_table[bra_ref[1, other_pair + t]].astype(F32)
        return carry

    lax.fori_loop(0, half, take_bra, 0)

    def take_ket(s, carry):
        spot = pl.ds(pl.multiple_of(s * SHELL, SHELL), SHELL)
        ket_one[spot, :] = mo_table[ket_ref[0, s]].astype(F32)
        ket_two[spot, :] = mo_table[ket_ref[1, s]].astype(F32)
        return carry

    lax.fori_loop(0, ket_ref.shape[1], take_ket, 0)

    depth = bra_one.shape[0]
    width = bra_t.shape[1]
    orbitals = bra_one.shape[1]
    row = iota((bra_t.shape[0], orbitals), 0)
    to_z_place = (z + ((row >> 4) & 7)) & (NZ - 1)
    to_y_place = (y + (row >> 7)) & (NY - 1)
    ab = to_z_place * 128 + c * 64 + to_y_place * 16 + (row & 15)
    orbital = iota((bra_t.shape[0], orbitals), 1)
    pick_a = where_one(orbital == ranges_ref[2] + (ab >> 5))
    pick_b = where_one(orbital == ranges_ref[3] + (ab & 31))
    small_a = dot_last(pick_a, bra_one[...].astype(BF)).astype(BF)
    small_b = dot_last(pick_b, bra_two[...].astype(BF)).astype(BF)
    source = iota((depth, width), 0)
    column = iota((depth, width), 1)
    over_m = where_one(source == (column >> 3))
    over_n = where_one(((source >> 3) == (column >> 6)) & ((source & 7) == (column & 7)))
    for start in range(0, bra_t.shape[0], 128):
        rows = slice(start, start + 128)
        bra_t[rows, :] = (dot(small_a[rows], over_m) * dot(small_b[rows], over_n)).astype(BF)

    pl.semaphore_wait(barrier, len(plane) + len(line))

    def ao_copy(p):
        return pltpu.make_async_remote_copy(
            ao_hbm.at[:, part_of(p)], ao_other.at[:, part_of(p)], core_send.at[p], core_recv.at[p],
            device_id=line_peer(0, 1), device_id_type=MESH,
        )

    mask_copy = pltpu.make_async_remote_copy(
        mask_ref, mask_other, core_send.at[PARTS], core_recv.at[PARTS], device_id=line_peer(0, 1), device_id_type=MESH
    )
    mask_copy.start()
    for p in range(PARTS):
        ao_copy(p).start()

    mask_spread = where_one(
        iota((mask_ref.shape[1], ao_own.shape[1]), 0) == (iota((mask_ref.shape[1], ao_own.shape[1]), 1) >> 6)
    )

    own_wide = dot(mask_ref[...].astype(F32).astype(BF), mask_spread)
    wide_other[0] = own_wide

    def screen(values, wide, p):
        factor = wide[:, part_of(p)].astype(BF)
        for t in range(half):
            block = slice(64 * t, 64 * t + 64)
            values[block, part_of(p)] = values[block, part_of(p)] * factor[t:t + 1, :]

    own_width = ao_own.shape[0]

    def own_part(p, carry):
        load_ao(p).wait()
        screen(ao_own, wide_other.at[0], p)
        for dy in range(NY):
            rows = slice(128 * dy, 128 * dy + 128)
            partial[rows, part_of(p)] = dot(bra_t[rows, :own_width], ao_own[:, part_of(p)])
        return carry

    lax.fori_loop(0, PARTS, own_part, 0)
    mask_copy.wait_recv()
    wide_other[1] = dot(mask_other[...].astype(F32).astype(BF), mask_spread)

    ways = (1, NY - 1)
    rows_y = NZ * OWN
    half_rows = (slice(0, rows_y // 2), slice(rows_y // 2, rows_y))

    def y_copy(p, way, part):
        return pltpu.make_async_remote_copy(
            to_y.at[p, way, part], from_y.at[p, way, part], y_send.at[p, way, part], y_recv.at[p, way, part],
            device_id=plane_peer(0, ways[way]), device_id_type=MESH,
        )

    def relay_copy(p, way):
        return pltpu.make_async_remote_copy(
            to_relay.at[p, way], from_relay.at[p, way], relay_send.at[p, way], relay_recv.at[p, way],
            device_id=plane_peer(0, ways[way]), device_id_type=MESH,
        )

    def other_part(p, carry):
        ao_copy(p).wait_recv()
        screen(ao_other, wide_other.at[1], p)
        for dy in (2, 1, 3, 0):
            rows = slice(rows_y * dy, rows_y * dy + rows_y)
            total = partial[rows, part_of(p)] + dot(bra_t[rows, own_width:], ao_other[:, part_of(p)])
            if dy == 0:
                own_sum[p] = total
            elif dy == 2:
                for way in range(2):
                    to_relay[p, way] = total[half_rows[way]].astype(BF)
                    relay_copy(p, way).start()
            else:
                way = ways.index(dy)
                kept[p, way] = total[half_rows[way]]
                to_y[p, way, 1 - way] = total[half_rows[1 - way]].astype(BF)
                y_copy(p, way, 1 - way).start()
        return carry

    def relay(p, carry):
        for way in range(2):
            relay_copy(p, way).wait_recv()
            to_y[p, way, way] = (kept[p, way] + from_relay[p, way].astype(F32)).astype(BF)
            y_copy(p, way, way).start()
        return carry

    def other_and_relay(p, carry):
        return relay(p - LAG, other_part(p, carry))

    lax.fori_loop(0, LAG, other_part, 0)
    lax.fori_loop(LAG, PARTS, other_and_relay, 0)

    columns = spread.shape[1]
    col = iota((orbitals, columns), 1)
    first = (((y + (col >> 8)) & (NY - 1)) << 4) + (((z + ((col >> 5) & 7)) & (NZ - 1)) << 1) + ((c + (col >> 4)) & 1)
    pick_i = where_one(iota((orbitals, columns), 0) == ranges_ref[0] + first)
    spread[...] = dot(ket_one[...].astype(BF), pick_i)
    j_row = iota((ket_narrow.shape[0], orbitals), 0)
    second = (((x + (j_row >> 4)) & (NX - 1)) << 4) + (j_row & 15)
    pick_j = where_one(iota((ket_narrow.shape[0], orbitals), 1) == ranges_ref[1] + second)
    narrow = dot_last(pick_j, ket_two[...].astype(BF)).astype(BF)
    ket_narrow[...] = jnp.concatenate([narrow, narrow], axis=1)

    def z_copy(p, dz):
        return pltpu.make_async_remote_copy(
            to_z.at[p, dz - 1], from_z.at[p, dz - 1], z_send.at[p, dz - 1], z_recv.at[p, dz - 1],
            device_id=line_peer(dz, 0), device_id_type=MESH,
        )

    def over_y(p):
        for way in range(2):
            for part in (1 - way, way):
                y_copy(p, way, part).wait_recv()
        for dz in (4, 3, 5, 2, 6, 1, 7, 0):
            part = own_sum[p, OWN * dz:OWN * dz + OWN]
            start = OWN * dz % (rows_y // 2)
            for way in range(2):
                part = part + from_y[p, way, 2 * dz // NZ, start:start + OWN].astype(F32)
            if dz:
                to_z[p, dz - 1] = part.astype(BF)
                z_copy(p, dz).start()
            else:
                own_z[p] = part

    lanes = where_one((iota((2 * OWN, 128), 0) & 15) == (iota((2 * OWN, 128), 1) & 15))

    def over_first(s, carry):
        sums = [None] * (columns // 128)
        factors = spread[pl.ds(pl.multiple_of(s * SHELL, SHELL), SHELL), :]
        for m in range(SHELL):
            block = ket_wide[pl.ds(pl.multiple_of((s * SHELL + m) * SHELL, SHELL), SHELL), :]
            for tile in range(columns // 128):
                term = factors[m:m + 1, 128 * tile:128 * tile + 128] * block
                sums[tile] = term if m == 0 else sums[tile] + term
        for tile in range(columns // 128):
            quarter[pl.ds(pl.multiple_of(s * SHELL, SHELL), SHELL), 128 * tile:128 * tile + 128] = sums[tile]
        return carry

    pairs = PART // (SHELL * SHELL)

    def over_z(p):
        summed = own_z[p]
        for dz in (1, 7, 2, 6, 3, 5, 4):
            z_copy(p, dz).wait_recv()
            summed = summed + from_z[p, dz - 1].astype(F32)
        high = summed.astype(BF)
        low = (summed - high.astype(F32)).astype(BF)
        ket_wide[part_of(p), :] = lax.dot_general(
            jnp.concatenate([high, low], axis=0), lanes, (((0,), (0,)), ((), ())), preferred_element_type=F32
        )
        lax.fori_loop(p * pairs, p * pairs + pairs, over_first, 0)

    def step(p, carry):
        over_y(p)
        return carry

    def both_steps(p, carry):
        over_y(p)
        over_z(p - 3)
        return carry

    def last_step(p, carry):
        over_z(p)
        return carry

    lax.fori_loop(PARTS - LAG, PARTS, relay, 0)
    lax.fori_loop(0, 3, step, 0)
    lax.fori_loop(3, PARTS, both_steps, 0)
    lax.fori_loop(PARTS - 3, PARTS, last_step, 0)
    value = quarter[...]
    value_high = value.astype(BF)
    value_low = (value - value_high.astype(F32)).astype(BF)
    both = dot(ket_narrow[...], jnp.concatenate([value_high, value_low], axis=0))

    def plane_copy(dx, dy, slot):
        return pltpu.make_async_remote_copy(
            to_xy.at[dx, dy], from_xy.at[slot[0], slot[1]], xy_send.at[dx * NY + dy], xy_recv.at[dx * NY + dy],
            device_id=plane_peer(dx, dy), device_id_type=MESH,
        )

    for dx, dy in sorted(plane, key=lambda d: -min(d[0], NX - d[0]) - min(d[1], NY - d[1])):
        to_xy[dx, dy] = both[16 * dx:16 * dx + 16, 256 * dy:256 * dy + 256].astype(BF)
        plane_copy(dx, dy, (y, x)).start()
    from_xy[y, x] = both[:16, :256].astype(BF)
    for dx, dy in plane:
        plane_copy(dx, dy, (lax.rem(y + NY - dy, NY), lax.rem(x + NX - dx, NX))).wait_recv()
    merged = [from_xy[k, 0].astype(F32) + from_xy[k, 1].astype(F32) + from_xy[k, 2].astype(F32) + from_xy[k, 3].astype(F32) for k in range(NY)]

    def line_copy(dz, dc, slot):
        return pltpu.make_async_remote_copy(
            to_zc.at[dz * NC + dc], from_zc.at[slot[0], slot[1]], zc_send.at[dz * NC + dc], zc_recv.at[dz * NC + dc],
            device_id=line_peer(dz, dc), device_id_type=MESH,
        )

    lane = iota((8, 128), 1)
    for dz, dc in sorted([(dz, dc) for dz in range(NZ) for dc in range(NC)], key=lambda d: -min(d[0], NZ - d[0])):
        group = dz * NC + dc
        tile = slice(128 * (group // 8), 128 * (group // 8) + 128)
        message = None
        for k in range(8):
            block = merged[k % 4][8 * (k // 4):8 * (k // 4) + 8, tile]
            shift = (16 * k - 16 * (group % 8)) % 128
            moved = pltpu.roll(block, shift, 1) if shift else block
            message = moved if message is None else jnp.where((lane >> 4) == k, moved, message)
        if group:
            to_zc[group] = message
            line_copy(dz, dc, (z, c)).start()
        else:
            from_zc[z, c] = message
    for dz, dc in line:
        line_copy(dz, dc, (lax.rem(z + NZ - dz, NZ), lax.rem(c + NC - dc, NC))).wait_recv()
    for k in range(NZ):
        left, right = from_zc[k, 0], from_zc[k, 1]
        out_ref[0:8, 128 * k:128 * k + 128] = jnp.where(lane < 64, left, pltpu.roll(right, 64, 1))
        out_ref[8:16, 128 * k:128 * k + 128] = jnp.where(lane < 64, pltpu.roll(left, 64, 1), right)

    mask_copy.wait_send()

    def drain(p, carry):
        ao_copy(p).wait_send()
        for way in range(2):
            relay_copy(p, way).wait_send()
            y_copy(p, way, 0).wait_send()
            y_copy(p, way, 1).wait_send()
        for dz in range(1, NZ):
            z_copy(p, dz).wait_send()
        return carry

    lax.fori_loop(0, PARTS, drain, 0)
    for dx, dy in plane:
        plane_copy(dx, dy, (y, x)).wait_send()
    for dz, dc in line:
        line_copy(dz, dc, (z, c)).wait_send()


def on_device(ao_ints, shell_mask, bra_shells, ket_shells, mo_coeff, mo_ranges):
    table = mo_coeff.reshape(mo_coeff.shape[0] // SHELL, SHELL, mo_coeff.shape[1])
    rows, cols = ao_ints.shape
    orbitals = mo_coeff.shape[1]
    ket_rows = ket_shells.shape[0] * SHELL
    bra_rows = NC * shell_mask.shape[0] * SHELL
    dma = pltpu.SemaphoreType.DMA
    whole = pl.BlockSpec(memory_space=pltpu.HBM)
    scalar = pl.BlockSpec(memory_space=pltpu.SMEM)
    vector = pl.BlockSpec(memory_space=pltpu.VMEM)
    return pl.pallas_call(
        kernel,
        out_shape=jax.ShapeDtypeStruct((16, 1024), F32),
        in_specs=[whole, vector, scalar, scalar, whole, scalar],
        out_specs=vector,
        scratch_shapes=[
            pltpu.VMEM((rows, cols), BF),
            pltpu.VMEM((rows, cols), BF),
            pltpu.VMEM(shell_mask.shape, jnp.int32),
            pltpu.VMEM(table.shape, BF),
            pltpu.VMEM((bra_rows, orbitals), F32),
            pltpu.VMEM((bra_rows, orbitals), F32),
            pltpu.VMEM((ket_rows, orbitals), F32),
            pltpu.VMEM((ket_rows, orbitals), F32),
            pltpu.VMEM((512, NC * rows), BF),
            pltpu.VMEM((512, cols), F32),
            pltpu.VMEM((PARTS, 2, 2, NZ * OWN // 2, PART), BF),
            pltpu.VMEM((PARTS, 2, 2, NZ * OWN // 2, PART), BF),
            pltpu.VMEM((PARTS, NZ - 1, OWN, PART), BF),
            pltpu.VMEM((PARTS, NZ - 1, OWN, PART), BF),
            pltpu.VMEM((PARTS, NZ * OWN, PART), F32),
            pltpu.VMEM((cols, 128), F32),
            pltpu.VMEM((64, 2 * ket_rows), BF),
            pltpu.VMEM((NC, shell_mask.shape[0], cols), F32),
            pltpu.VMEM((PARTS, OWN, PART), F32),
            pltpu.VMEM((PARTS, 2, NZ * OWN // 2, PART), BF),
            pltpu.VMEM((PARTS, 2, NZ * OWN // 2, PART), BF),
            pltpu.VMEM((PARTS, 2, NZ * OWN // 2, PART), F32),
            pltpu.VMEM((ket_rows, 1024), F32),
            pltpu.VMEM((ket_rows, 1024), F32),
            pltpu.VMEM((NX, NY, 16, 256), BF),
            pltpu.VMEM((NY, NX, 16, 256), BF),
            pltpu.VMEM((NZ * NC, 8, 128), F32),
            pltpu.VMEM((NZ, NC, 8, 128), F32),
            dma((PARTS + 1,)),
            dma((PARTS + 1,)),
            dma((PARTS + 1,)),
            dma((PARTS, 2, 2)),
            dma((PARTS, 2, 2)),
            dma((PARTS, 2)),
            dma((PARTS, 2)),
            dma((PARTS, NZ - 1)),
            dma((PARTS, NZ - 1)),
            dma((NX * NY,)),
            dma((NX * NY,)),
            dma((NZ * NC,)),
            dma((NZ * NC,)),
        ],
        compiler_params=pltpu.CompilerParams(collective_id=0, has_side_effects=True, vmem_limit_bytes=67_043_328),
    )(ao_ints, shell_mask, bra_shells.T, ket_shells.T, table, mo_ranges)


def solution(mesh):
    return jax.shard_map(
        on_device,
        mesh=mesh,
        in_specs=(P("pair", "batch"), P("pair", "batch"), P(), P("batch", None), P(), P()),
        out_specs=P(("pair", "batch"), None),
        check_vma=False,
    )
```

```python
import jax
import jax.numpy as jnp
from jax import lax
from jax.experimental import pallas as pl
from jax.experimental.pallas import tpu as pltpu
from jax.sharding import PartitionSpec as P

SHELL = 8
NX, NY, NZ, NC = 4, 4, 8, 2
OWN = 16
PARTS, PART = 4, 256
LAG = 2
MESH = pl.DeviceIdType.MESH
BF = jnp.bfloat16
F32 = jnp.float32


def iota(shape, dim):
    return lax.broadcasted_iota(jnp.int32, shape, dim)


def where_one(condition):
    return jnp.where(condition, 1.0, 0.0).astype(BF)


def dot(a, b):
    return jnp.dot(a, b, preferred_element_type=F32)


def dot_last(a, b):
    return lax.dot_general(a, b, (((1,), (1,)), ((), ())), preferred_element_type=F32)


def pair_id(y, z, c):
    return (y * NZ + z) * NC + c


def kernel(
    ao_hbm, mask_ref, bra_ref, ket_ref, mo_hbm, ranges_ref, out_ref,
    ao_own, ao_other, mask_other, mo_table, bra_one, bra_two, ket_one, ket_two,
    bra_t, partial, to_y, from_y, to_z, from_z, own_sum, ket_wide, ket_narrow,
    wide_other, own_z, to_relay, from_relay, kept, spread, quarter, to_xy, from_xy, to_zc, from_zc,
    load_sem, core_send, core_recv, y_send, y_recv, relay_send, relay_recv, z_send, z_recv, xy_send, xy_recv, zc_send, zc_recv,
):
    place = lax.axis_index("pair")
    x = lax.axis_index("batch")
    c = lax.rem(place, NC)
    z = lax.rem(place // NC, NZ)
    y = place // (NC * NZ)

    def plane_peer(dx, dy):
        return (pair_id(lax.rem(y + dy, NY), z, c), lax.rem(x + dx, NX))

    def line_peer(dz, dc):
        return (pair_id(y, lax.rem(z + dz, NZ), lax.rem(c + dc, NC)), x)

    def part_of(p):
        return pl.ds(pl.multiple_of(p * PART, PART), PART)

    def load_ao(p):
        return pltpu.make_async_copy(ao_hbm.at[:, part_of(p)], ao_own.at[:, part_of(p)], load_sem.at[p])

    load_mo = pltpu.make_async_copy(mo_hbm, mo_table, load_sem.at[PARTS])
    load_mo.start()
    for p in range(PARTS):
        load_ao(p).start()
    barrier = pltpu.get_barrier_semaphore()
    plane = [(dx, dy) for dx in range(NX) for dy in range(NY) if dx or dy]
    line = [(dz, dc) for dz in range(NZ) for dc in range(NC) if dz or dc]
    for dx, dy in plane:
        pl.semaphore_signal(barrier, inc=1, device_id=plane_peer(dx, dy), device_id_type=MESH)
    for dz, dc in line:
        pl.semaphore_signal(barrier, inc=1, device_id=line_peer(dz, dc), device_id_type=MESH)

    load_mo.wait()
    half = mask_ref.shape[0]
    first_pair = place * half
    other_pair = pair_id(y, z, lax.rem(c + 1, NC)) * half

    def take_bra(t, carry):
        spot = pl.ds(pl.multiple_of(t * SHELL, SHELL), SHELL)
        late = pl.ds(pl.multiple_of((half + t) * SHELL, SHELL), SHELL)
        bra_one[spot, :] = mo_table[bra_ref[0, first_pair + t]].astype(F32)
        bra_two[spot, :] = mo_table[bra_ref[1, first_pair + t]].astype(F32)
        bra_one[late, :] = mo_table[bra_ref[0, other_pair + t]].astype(F32)
        bra_two[late, :] = mo_table[bra_ref[1, other_pair + t]].astype(F32)
        return carry

    lax.fori_loop(0, half, take_bra, 0)

    def take_ket(s, carry):
        spot = pl.ds(pl.multiple_of(s * SHELL, SHELL), SHELL)
        ket_one[spot, :] = mo_table[ket_ref[0, s]].astype(F32)
        ket_two[spot, :] = mo_table[ket_ref[1, s]].astype(F32)
        return carry

    lax.fori_loop(0, ket_ref.shape[1], take_ket, 0)

    depth = bra_one.shape[0]
    width = bra_t.shape[1]
    orbitals = bra_one.shape[1]
    row = iota((bra_t.shape[0], orbitals), 0)
    to_z_place = (z + ((row >> 4) & 7)) & (NZ - 1)
    to_y_place = (y + (row >> 7)) & (NY - 1)
    ab = to_z_place * 128 + c * 64 + to_y_place * 16 + (row & 15)
    orbital = iota((bra_t.shape[0], orbitals), 1)
    pick_a = where_one(orbital == ranges_ref[2] + (ab >> 5))
    pick_b = where_one(orbital == ranges_ref[3] + (ab & 31))
    small_a = dot_last(pick_a, bra_one[...].astype(BF)).astype(BF)
    small_b = dot_last(pick_b, bra_two[...].astype(BF)).astype(BF)
    source = iota((depth, width), 0)
    column = iota((depth, width), 1)
    over_m = where_one(source == (column >> 3))
    over_n = where_one(((source >> 3) == (column >> 6)) & ((source & 7) == (column & 7)))
    for start in range(0, bra_t.shape[0], 128):
        rows = slice(start, start + 128)
        bra_t[rows, :] = (dot(small_a[rows], over_m) * dot(small_b[rows], over_n)).astype(BF)

    pl.semaphore_wait(barrier, len(plane) + len(line))

    def ao_copy(p):
        return pltpu.make_async_remote_copy(
            ao_hbm.at[:, part_of(p)], ao_other.at[:, part_of(p)], core_send.at[p], core_recv.at[p],
            device_id=line_peer(0, 1), device_id_type=MESH,
        )

    mask_copy = pltpu.make_async_remote_copy(
        mask_ref, mask_other, core_send.at[PARTS], core_recv.at[PARTS], device_id=line_peer(0, 1), device_id_type=MESH
    )
    mask_copy.start()
    for p in range(PARTS):
        ao_copy(p).start()

    mask_spread = where_one(
        iota((mask_ref.shape[1], ao_own.shape[1]), 0) == (iota((mask_ref.shape[1], ao_own.shape[1]), 1) >> 6)
    )

    own_wide = dot(mask_ref[...].astype(F32).astype(BF), mask_spread)
    wide_other[0] = own_wide

    def screen(values, wide, p):
        factor = wide[:, part_of(p)].astype(BF)
        for t in range(half):
            block = slice(64 * t, 64 * t + 64)
            values[block, part_of(p)] = values[block, part_of(p)] * factor[t:t + 1, :]

    own_width = ao_own.shape[0]

    def own_part(p, carry):
        load_ao(p).wait()
        screen(ao_own, wide_other.at[0], p)
        for dy in range(NY):
            rows = slice(128 * dy, 128 * dy + 128)
            partial[rows, part_of(p)] = dot(bra_t[rows, :own_width], ao_own[:, part_of(p)])
        return carry

    lax.fori_loop(0, PARTS, own_part, 0)

    columns = spread.shape[1]
    col = iota((orbitals, columns), 1)
    first = (((y + (col >> 8)) & (NY - 1)) << 4) + (((z + ((col >> 5) & 7)) & (NZ - 1)) << 1) + ((c + (col >> 4)) & 1)
    pick_i = where_one(iota((orbitals, columns), 0) == ranges_ref[0] + first)
    spread[...] = dot(ket_one[...].astype(BF), pick_i)
    j_row = iota((ket_narrow.shape[0], orbitals), 0)
    second = (((x + (j_row >> 4)) & (NX - 1)) << 4) + (j_row & 15)
    pick_j = where_one(iota((ket_narrow.shape[0], orbitals), 1) == ranges_ref[1] + second)
    narrow = dot_last(pick_j, ket_two[...].astype(BF)).astype(BF)
    ket_narrow[...] = jnp.concatenate([narrow, narrow], axis=1)

    mask_copy.wait_recv()
    wide_other[1] = dot(mask_other[...].astype(F32).astype(BF), mask_spread)

    ways = (1, NY - 1)
    rows_y = NZ * OWN
    half_rows = (slice(0, rows_y // 2), slice(rows_y // 2, rows_y))

    def y_copy(p, way, part):
        return pltpu.make_async_remote_copy(
            to_y.at[p, way, part], from_y.at[p, way, part], y_send.at[p, way, part], y_recv.at[p, way, part],
            device_id=plane_peer(0, ways[way]), device_id_type=MESH,
        )

    def relay_copy(p, way):
        return pltpu.make_async_remote_copy(
            to_relay.at[p, way], from_relay.at[p, way], relay_send.at[p, way], relay_recv.at[p, way],
            device_id=plane_peer(0, ways[way]), device_id_type=MESH,
        )

    def other_part(p, carry):
        ao_copy(p).wait_recv()
        screen(ao_other, wide_other.at[1], p)
        for dy in (2, 1, 3, 0):
            rows = slice(rows_y * dy, rows_y * dy + rows_y)
            total = partial[rows, part_of(p)] + dot(bra_t[rows, own_width:], ao_other[:, part_of(p)])
            if dy == 0:
                own_sum[p] = total
            elif dy == 2:
                for way in range(2):
                    to_relay[p, way] = total[half_rows[way]].astype(BF)
                    relay_copy(p, way).start()
            else:
                way = ways.index(dy)
                kept[p, way] = total[half_rows[way]]
                to_y[p, way, 1 - way] = total[half_rows[1 - way]].astype(BF)
                y_copy(p, way, 1 - way).start()
        return carry

    def relay(p, carry):
        for way in range(2):
            relay_copy(p, way).wait_recv()
            to_y[p, way, way] = (kept[p, way] + from_relay[p, way].astype(F32)).astype(BF)
            y_copy(p, way, way).start()
        return carry

    def other_and_relay(p, carry):
        return relay(p - LAG, other_part(p, carry))

    lax.fori_loop(0, LAG, other_part, 0)
    lax.fori_loop(LAG, PARTS, other_and_relay, 0)

    def z_copy(p, dz):
        return pltpu.make_async_remote_copy(
            to_z.at[p, dz - 1], from_z.at[p, dz - 1], z_send.at[p, dz - 1], z_recv.at[p, dz - 1],
            device_id=line_peer(dz, 0), device_id_type=MESH,
        )

    def over_y(p):
        for way in range(2):
            for part in (1 - way, way):
                y_copy(p, way, part).wait_recv()
        for dz in (4, 3, 5, 2, 6, 1, 7, 0):
            part = own_sum[p, OWN * dz:OWN * dz + OWN]
            start = OWN * dz % (rows_y // 2)
            for way in range(2):
                part = part + from_y[p, way, 2 * dz // NZ, start:start + OWN].astype(F32)
            if dz:
                to_z[p, dz - 1] = part.astype(BF)
                z_copy(p, dz).start()
            else:
                own_z[p] = part

    lanes = where_one((iota((2 * OWN, 128), 0) & 15) == (iota((2 * OWN, 128), 1) & 15))

    def over_first(s, carry):
        sums = [None] * (columns // 128)
        factors = spread[pl.ds(pl.multiple_of(s * SHELL, SHELL), SHELL), :]
        for m in range(SHELL):
            block = ket_wide[pl.ds(pl.multiple_of((s * SHELL + m) * SHELL, SHELL), SHELL), :]
            for tile in range(columns // 128):
                term = factors[m:m + 1, 128 * tile:128 * tile + 128] * block
                sums[tile] = term if m == 0 else sums[tile] + term
        for tile in range(columns // 128):
            quarter[pl.ds(pl.multiple_of(s * SHELL, SHELL), SHELL), 128 * tile:128 * tile + 128] = sums[tile]
        return carry

    pairs = PART // (SHELL * SHELL)

    def over_z(p):
        summed = own_z[p]
        for dz in (1, 7, 2, 6, 3, 5, 4):
            z_copy(p, dz).wait_recv()
            summed = summed + from_z[p, dz - 1].astype(F32)
        high = summed.astype(BF)
        low = (summed - high.astype(F32)).astype(BF)
        ket_wide[part_of(p), :] = lax.dot_general(
            jnp.concatenate([high, low], axis=0), lanes, (((0,), (0,)), ((), ())), preferred_element_type=F32
        )
        lax.fori_loop(p * pairs, p * pairs + pairs, over_first, 0)

    def step(p, carry):
        over_y(p)
        return carry

    def both_steps(p, carry):
        over_y(p)
        over_z(p - 3)
        return carry

    def last_step(p, carry):
        over_z(p)
        return carry

    lax.fori_loop(PARTS - LAG, PARTS, relay, 0)
    lax.fori_loop(0, 3, step, 0)
    lax.fori_loop(3, PARTS, both_steps, 0)
    lax.fori_loop(PARTS - 3, PARTS, last_step, 0)
    value = quarter[...]
    value_high = value.astype(BF)
    value_low = (value - value_high.astype(F32)).astype(BF)
    both = dot(ket_narrow[...], jnp.concatenate([value_high, value_low], axis=0))

    def plane_copy(dx, dy, slot):
        return pltpu.make_async_remote_copy(
            to_xy.at[dx, dy], from_xy.at[slot[0], slot[1]], xy_send.at[dx * NY + dy], xy_recv.at[dx * NY + dy],
            device_id=plane_peer(dx, dy), device_id_type=MESH,
        )

    for dx, dy in sorted(plane, key=lambda d: -min(d[0], NX - d[0]) - min(d[1], NY - d[1])):
        to_xy[dx, dy] = both[16 * dx:16 * dx + 16, 256 * dy:256 * dy + 256].astype(BF)
        plane_copy(dx, dy, (y, x)).start()
    from_xy[y, x] = both[:16, :256].astype(BF)
    for dx, dy in plane:
        plane_copy(dx, dy, (lax.rem(y + NY - dy, NY), lax.rem(x + NX - dx, NX))).wait_recv()
    merged = [from_xy[k, 0].astype(F32) + from_xy[k, 1].astype(F32) + from_xy[k, 2].astype(F32) + from_xy[k, 3].astype(F32) for k in range(NY)]

    def line_copy(dz, dc, slot):
        return pltpu.make_async_remote_copy(
            to_zc.at[dz * NC + dc], from_zc.at[slot[0], slot[1]], zc_send.at[dz * NC + dc], zc_recv.at[dz * NC + dc],
            device_id=line_peer(dz, dc), device_id_type=MESH,
        )

    lane = iota((8, 128), 1)
    for dz, dc in sorted([(dz, dc) for dz in range(NZ) for dc in range(NC)], key=lambda d: -min(d[0], NZ - d[0])):
        group = dz * NC + dc
        tile = slice(128 * (group // 8), 128 * (group // 8) + 128)
        message = None
        for k in range(8):
            block = merged[k % 4][8 * (k // 4):8 * (k // 4) + 8, tile]
            shift = (16 * k - 16 * (group % 8)) % 128
            moved = pltpu.roll(block, shift, 1) if shift else block
            message = moved if message is None else jnp.where((lane >> 4) == k, moved, message)
        if group:
            to_zc[group] = message
            line_copy(dz, dc, (z, c)).start()
        else:
            from_zc[z, c] = message
    for dz, dc in line:
        line_copy(dz, dc, (lax.rem(z + NZ - dz, NZ), lax.rem(c + NC - dc, NC))).wait_recv()
    for k in range(NZ):
        left, right = from_zc[k, 0], from_zc[k, 1]
        out_ref[0:8, 128 * k:128 * k + 128] = jnp.where(lane < 64, left, pltpu.roll(right, 64, 1))
        out_ref[8:16, 128 * k:128 * k + 128] = jnp.where(lane < 64, pltpu.roll(left, 64, 1), right)

    mask_copy.wait_send()

    def drain(p, carry):
        ao_copy(p).wait_send()
        for way in range(2):
            relay_copy(p, way).wait_send()
            y_copy(p, way, 0).wait_send()
            y_copy(p, way, 1).wait_send()
        for dz in range(1, NZ):
            z_copy(p, dz).wait_send()
        return carry

    lax.fori_loop(0, PARTS, drain, 0)
    for dx, dy in plane:
        plane_copy(dx, dy, (y, x)).wait_send()
    for dz, dc in line:
        line_copy(dz, dc, (z, c)).wait_send()


def on_device(ao_ints, shell_mask, bra_shells, ket_shells, mo_coeff, mo_ranges):
    table = mo_coeff.reshape(mo_coeff.shape[0] // SHELL, SHELL, mo_coeff.shape[1])
    rows, cols = ao_ints.shape
    orbitals = mo_coeff.shape[1]
    ket_rows = ket_shells.shape[0] * SHELL
    bra_rows = NC * shell_mask.shape[0] * SHELL
    dma = pltpu.SemaphoreType.DMA
    whole = pl.BlockSpec(memory_space=pltpu.HBM)
    scalar = pl.BlockSpec(memory_space=pltpu.SMEM)
    vector = pl.BlockSpec(memory_space=pltpu.VMEM)
    return pl.pallas_call(
        kernel,
        out_shape=jax.ShapeDtypeStruct((16, 1024), F32),
        in_specs=[whole, vector, scalar, scalar, whole, scalar],
        out_specs=vector,
        scratch_shapes=[
            pltpu.VMEM((rows, cols), BF),
            pltpu.VMEM((rows, cols), BF),
            pltpu.VMEM(shell_mask.shape, jnp.int32),
            pltpu.VMEM(table.shape, BF),
            pltpu.VMEM((bra_rows, orbitals), F32),
            pltpu.VMEM((bra_rows, orbitals), F32),
            pltpu.VMEM((ket_rows, orbitals), F32),
            pltpu.VMEM((ket_rows, orbitals), F32),
            pltpu.VMEM((512, NC * rows), BF),
            pltpu.VMEM((512, cols), F32),
            pltpu.VMEM((PARTS, 2, 2, NZ * OWN // 2, PART), BF),
            pltpu.VMEM((PARTS, 2, 2, NZ * OWN // 2, PART), BF),
            pltpu.VMEM((PARTS, NZ - 1, OWN, PART), BF),
            pltpu.VMEM((PARTS, NZ - 1, OWN, PART), BF),
            pltpu.VMEM((PARTS, NZ * OWN, PART), F32),
            pltpu.VMEM((cols, 128), F32),
            pltpu.VMEM((64, 2 * ket_rows), BF),
            pltpu.VMEM((NC, shell_mask.shape[0], cols), F32),
            pltpu.VMEM((PARTS, OWN, PART), F32),
            pltpu.VMEM((PARTS, 2, NZ * OWN // 2, PART), BF),
            pltpu.VMEM((PARTS, 2, NZ * OWN // 2, PART), BF),
            pltpu.VMEM((PARTS, 2, NZ * OWN // 2, PART), F32),
            pltpu.VMEM((ket_rows, 1024), F32),
            pltpu.VMEM((ket_rows, 1024), F32),
            pltpu.VMEM((NX, NY, 16, 256), BF),
            pltpu.VMEM((NY, NX, 16, 256), BF),
            pltpu.VMEM((NZ * NC, 8, 128), F32),
            pltpu.VMEM((NZ, NC, 8, 128), F32),
            dma((PARTS + 1,)),
            dma((PARTS + 1,)),
            dma((PARTS + 1,)),
            dma((PARTS, 2, 2)),
            dma((PARTS, 2, 2)),
            dma((PARTS, 2)),
            dma((PARTS, 2)),
            dma((PARTS, NZ - 1)),
            dma((PARTS, NZ - 1)),
            dma((NX * NY,)),
            dma((NX * NY,)),
            dma((NZ * NC,)),
            dma((NZ * NC,)),
        ],
        compiler_params=pltpu.CompilerParams(collective_id=0, has_side_effects=True, vmem_limit_bytes=67_043_328),
    )(ao_ints, shell_mask, bra_shells.T, ket_shells.T, table, mo_ranges)


def solution(mesh):
    return jax.shard_map(
        on_device,
        mesh=mesh,
        in_specs=(P("pair", "batch"), P("pair", "batch"), P(), P("batch", None), P(), P()),
        out_specs=P(("pair", "batch"), None),
        check_vma=False,
    )
```
